512 devices in a mesh: ex: 64 (over y_lo, z, core), hid: 8 (over x, y_hi).
Axes of the slice: x: 4, y: 4 (y_hi: 2, y_lo: 2; y = y_hi * 2 + y_lo), z: 16, core: 2. Of those that a mesh axis runs over, the one named last changes fastest.
Arguments:
- activations: bfloat16 [256, 192, 14336], P('ex', None, 'hid'), may hold values from -6 to 6
- out_grads: bfloat16 [256, 192, 4096], P('ex', None, 'hid'), may hold values from -6 to 6
- token_mask: int32 [256, 192], P('ex'), may hold values from 0 to 1, as said below
- proj_in: bfloat16 [14336, 64], P('hid'), may hold values from -0.046875 to 0.046875
- proj_out: bfloat16 [4096, 64], P('hid'), may hold values from -0.09375 to 0.09375
- inv_input: float32 [64, 64], replicated, as said below
- inv_output: float32 [64, 64], replicated, as said below
- query_feats: bfloat16 [4096, 4096], P('ex', 'hid'), may hold values from -6 to 6
Outputs:
- scores: float32 [4096, 256], P('ex', 'hid')
The draws below stay inside these ranges and needn't reach their ends.
Inputs may be any that keep to these rules, and one draw needn't show every extreme that they name: `token_mask`: each row is 48 or more ones followed by zeros; some row is all ones. `inv_input`: symmetric. `inv_output`: symmetric.
All inputs are finite; a program needn't handle non-finite values.
Results may differ from the reference program's by a relative error of at most 0.0041.
Values may be sent and summed in bfloat16 or wider, within the bound.
A program may use at most 64 MiB of HBM per device.

```python
import math
import jax
import jax.numpy as jnp
from jax import lax

D = 4096
FF = 14336
RANK = 64
LEN = 192
TRAIN = 256
QUERIES = 4096
FEAT = 4096


def symmetric_factor(key):
    key_diag, key_off = jax.random.split(key)
    diag_vals = 1.0 + jax.random.uniform(key_diag, (RANK,), jnp.float32)
    noise = jax.random.normal(key_off, (RANK, RANK), jnp.float32)
    sym_noise = (noise + noise.T) * (0.4 / math.sqrt(2.0 * RANK))
    eye_mat = jnp.eye(RANK, dtype=jnp.float32)
    return sym_noise * (1.0 - eye_mat) + eye_mat * diag_vals[None, :]


def draw_inv_input(key, part):
    return symmetric_factor(jax.random.fold_in(key, 11))


def draw_inv_output(key, part):
    return symmetric_factor(jax.random.fold_in(key, 23))


def draw_token_mask(key, part):
    key_len, key_full = jax.random.split(jax.random.fold_in(key, 5))
    lengths = jax.random.randint(key_len, (TRAIN,), LEN // 4, LEN + 1)
    full_pick = jax.random.randint(key_full, (TRAIN,), 0, 4)
    lengths = jnp.where(full_pick == 0, LEN, lengths)
    lengths = lengths.at[0].set(LEN)
    positions = jnp.arange(LEN, dtype=jnp.int32)
    return (positions[None, :] < lengths[:, None]).astype(jnp.int32)


def block_levels(own_key, dims, shards, low, top_value):
    level, own = 1.0, jax.random.fold_in(own_key, 6)
    for axis_at, shards_of in shards:
        draws = jnp.exp(jax.random.uniform(jax.random.fold_in(own, axis_at), (shards_of,), jnp.float32, low / len(shards), top_value / len(shards)))
        level = level * jnp.repeat(draws, dims[axis_at] // shards_of).reshape([-1 if axis == axis_at else 1 for axis in range(len(dims))])
    return level


def gaussian(key, extent, deviation, reach, cuts=(), kind=jnp.bfloat16):
    values = deviation * jax.random.normal(key, extent, jnp.float32)
    if cuts:
        values = values * block_levels(key, extent, cuts, -0.22, 0.18)
    return jnp.clip(values, -reach, reach).astype(kind)


def setup_inputs(seed: int = 0) -> dict:
    arg_keys = jax.random.split(jax.random.key(seed), 9)
    return {
        "activations": gaussian(arg_keys[0], (TRAIN, LEN, FF), 1.0, 6.0, ((0, 64), (2, 8))),
        "out_grads": gaussian(arg_keys[1], (TRAIN, LEN, D), 1.0, 6.0, ((0, 64), (2, 8))),
        "token_mask": draw_token_mask(jax.random.fold_in(arg_keys[8], 71), 0),
        "proj_in": gaussian(arg_keys[3], (FF, RANK), FF ** -0.5, 0.046875, ((0, 8),)),
        "proj_out": gaussian(arg_keys[4], (D, RANK), D ** -0.5, 0.09375, ((0, 8),)),
        "inv_input": draw_inv_input(jax.random.fold_in(arg_keys[8], 71), 0),
        "inv_output": draw_inv_output(jax.random.fold_in(arg_keys[8], 71), 0),
        "query_feats": gaussian(arg_keys[7], (QUERIES, FEAT), 1.0, 6.0, ((0, 64), (1, 8))),
    }


def reference(activations, out_grads, token_mask, proj_in, proj_out, inv_input, inv_output, query_feats):
    in_side = jnp.dot(activations.reshape(TRAIN * LEN, FF), proj_in, preferred_element_type=jnp.float32)
    in_pre = jnp.dot(in_side, inv_input, precision=lax.Precision.HIGHEST)
    out_side = jnp.dot(out_grads.reshape(TRAIN * LEN, D), proj_out, preferred_element_type=jnp.float32)
    weights = token_mask.astype(jnp.float32)
    counted = jnp.sum(weights, axis=1)
    masked = in_pre.reshape(TRAIN, LEN, RANK) * weights[:, :, None]
    outer = jnp.einsum("slr,slq->srq", masked, out_side.reshape(TRAIN, LEN, RANK), precision=lax.Precision.HIGHEST)
    train_feats = (outer / counted[:, None, None]).astype(jnp.bfloat16).reshape(TRAIN, FEAT)
    queries = query_feats.reshape(QUERIES, RANK, RANK).astype(jnp.float32)
    query_pre = jnp.einsum("qij,jk->qik", queries, inv_output, precision=lax.Precision.HIGHEST)
    query_pre = query_pre.astype(jnp.bfloat16).reshape(QUERIES, FEAT)
    return jnp.dot(query_pre, train_feats.T, preferred_element_type=jnp.float32)
```

```python
import functools

import jax
import jax.numpy as jnp
from jax import lax
from jax.experimental import pallas as pl
from jax.experimental.pallas import tpu as pltpu
from jax.sharding import PartitionSpec as P

MESH = pl.DeviceIdType.MESH
F32 = jnp.float32
BF16 = jnp.bfloat16
SEND = jnp.float32
NT = (((1,), (1,)), ((), ()))
TN = (((0,), (0,)), ((), ()))
HIGHEST = lax.Precision.HIGHEST


def iota(shape, dim):
    return lax.broadcasted_iota(jnp.int32, shape, dim)


def kernel(
    act, grads, mask, proj_in, proj_out, inv_in, inv_out, query, out,
    act_v, grads_v, mask_v, win_v, wout_v, invin_v, invout_v, query_v,
    part, recv1, spread, qsend, qall, perm, feat, recv2, score, recv3, rows,
    in_sem, send1, got1, sendq, gotq, send2, got2, send3, got3,
):
    ex, hid = lax.axis_index("ex"), lax.axis_index("hid")
    ylo, z, core = ex // 32, (ex // 2) % 16, ex % 2
    x, yhi = hid // 2, hid % 2
    plane = (ylo * 2 + core) * 8 + hid

    def at_plane(p):
        return ((p // 16) * 32 + z * 2 + (p // 8) % 2, p % 8)

    def at_z(z2):
        return (ylo * 32 + z2 * 2 + core, hid)

    copies = []

    def load(src, dst):
        copy = pltpu.make_async_copy(src, dst, in_sem.at[len(copies)])
        copy.start()
        copies.append(copy)
        return copy

    w_loads = [load(proj_in, win_v.at[pl.ds(64 * k, 64)]) for k in range(2)]
    a_loads, g_loads = [], []
    a_loads.append(load(act.at[0], act_v.at[0]))
    for half in range(2):
        for group in range(4):
            w_loads.append(
                load(proj_out.at[pl.ds(32 * half, 32)], wout_v.at[pl.ds(128 * half + 32 * group, 32)])
            )
    g_loads.append(load(grads.at[0], grads_v.at[0]))
    for s in range(1, 4):
        a_loads.append(load(act.at[s], act_v.at[s]))
        g_loads.append(load(grads.at[s], grads_v.at[s]))
    late = [load(query, query_v), load(inv_in, invin_v), load(inv_out, invout_v), load(mask, mask_v)]

    barrier = pltpu.get_barrier_semaphore()
    for d in range(1, 32):
        pl.semaphore_signal(barrier, inc=1, device_id=at_plane((plane + d) % 32), device_id_type=MESH)
    for d in range(1, 16):
        pl.semaphore_signal(barrier, inc=1, device_id=at_z((z + d) % 16), device_id_type=MESH)

    for copy in w_loads:
        copy.wait()
    lane48 = iota((48, 128), 1)
    lane96 = iota((96, 128), 1)
    for s in range(4):
        a_loads[s].wait()
        y = lax.dot_general(act_v[s], win_v[...], NT, preferred_element_type=F32)
        packed = jnp.where(lane96 < 64, y[:96], y[96:]).astype(SEND)
        g_loads[s].wait()
        o = lax.dot_general(grads_v[s], wout_v[...], NT, preferred_element_type=F32)
        for half in range(2):
            c = o[:, 128 * half : 128 * half + 128]
            picked = jnp.where(
                lane48 < 64,
                jnp.where(lane48 < 32, c[:48], c[48:96]),
                jnp.where(lane48 < 96, c[96:144], c[144:]),
            )
            part[2 * s + half, :96] = packed
            part[2 * s + half, 96:] = picked.astype(SEND)

    pl.semaphore_wait(barrier, 46)

    def copy1(d):
        to = (hid + d) % 8
        return pltpu.make_async_remote_copy(
            part.at[to], recv1.at[d - 1], send1.at[d - 1], got1, device_id=(ex, to), device_id_type=MESH
        )

    for d in range(1, 8):
        copy1(d).start()

    for copy in late:
        copy.wait()
    m, col = iota((64, 128), 0), iota((64, 128), 1)
    place = m == 32 * (col // 64) + col % 32
    even = jnp.where(place & ((col // 32) % 2 == 0), 1.0, 0.0).astype(F32)
    odd = jnp.where(place & ((col // 32) % 2 == 1), 1.0, 0.0).astype(F32)
    both = jnp.concatenate(
        [
            jnp.dot(invout_v[...], even, precision=HIGHEST, preferred_element_type=F32),
            jnp.dot(invout_v[...], odd, precision=HIGHEST, preferred_element_type=F32),
        ],
        axis=0,
    )
    pre = [
        jnp.dot(
            query_v[:, 128 * b : 128 * b + 128].astype(F32), both, precision=HIGHEST, preferred_element_type=F32
        )
        for b in range(4)
    ]
    lane64 = iota((64, 128), 1)
    for b in range(2):
        left, right = pre[2 * b], pre[2 * b + 1]
        cols = slice(128 * b, 128 * b + 128)
        qsend[0, :, cols] = jnp.where(lane64 < 64, left, pltpu.roll(right, 64, 1)).astype(BF16)
        qsend[1, :, cols] = jnp.where(lane64 < 64, pltpu.roll(left, 64, 1), right).astype(BF16)
    my_rows = pl.ds(pl.multiple_of((ylo * 2 + core) * 64, 64), 64)

    def copyq(d):
        to = (plane + d) % 32
        return pltpu.make_async_remote_copy(
            qsend.at[to % 2], qall.at[hid, my_rows], sendq.at[d - 1], gotq, device_id=at_plane(to), device_id_type=MESH
        )

    for d in range(1, 32):
        copyq(d).start()
    pltpu.make_async_copy(qsend.at[yhi], qall.at[hid, my_rows], gotq).start()

    i, f = iota((64, 128), 0), iota((64, 128), 1)
    for k in range(16):
        pick = jnp.where(i == 4 * k + f // 32, 1.0, 0.0).astype(F32)
        spread[k] = jnp.dot(invin_v[...], pick, precision=HIGHEST, preferred_element_type=F32)
    r, c = iota((512, 256), 0), iota((512, 256), 1)
    take = (c % 16 == r // 32) & (r % 8 < 4) & (c // 16 == 4 * ((r // 8) % 4) + r % 8)
    perm[...] = jnp.where(take, 1.0, 0.0).astype(BF16)
    mask_row = mask_v[pl.ds(x, 1), :].astype(F32)
    count = jnp.sum(mask_row, axis=1, keepdims=True)
    t0, t1 = iota((48, 192), 0), iota((48, 192), 1)
    chosen = jnp.where(t1 % 48 == t0, 1.0, 0.0).astype(F32) * mask_row
    u0, u1 = iota((192, 128), 0), iota((192, 128), 1)
    group_of = jnp.where(u0 // 48 == u1 // 32, 1.0, 0.0).astype(BF16)
    weight = jnp.dot(chosen.astype(BF16), group_of, preferred_element_type=F32)

    pltpu.make_async_copy(recv1, recv1, got1).wait()
    total = part[hid].astype(F32)
    for d in range(7):
        total = total + recv1[d].astype(F32)
    side_in = total[:96]
    side_out = total[96:] * weight
    in_hi = side_in.astype(BF16)
    in_lo = (side_in - in_hi.astype(F32)).astype(BF16)
    out_hi = side_out.astype(BF16)
    out_lo = (side_out - out_hi.astype(F32)).astype(BF16)
    right = jnp.concatenate([out_hi, out_lo, out_hi], axis=0)
    first = lax.dot_general(
        jnp.concatenate([in_hi[:48], in_hi[:48], in_lo[:48]], axis=0), right, TN, preferred_element_type=F32
    )
    second = lax.dot_general(
        jnp.concatenate([in_hi[48:], in_hi[48:], in_lo[48:]], axis=0), right, TN, preferred_element_type=F32
    )
    outer = jnp.where(
        lane64 < 64,
        jnp.where(lane64 < 32, first[:64], second[:64]),
        jnp.where(lane64 < 96, first[64:], second[64:]),
    )
    outer = outer + pltpu.roll(outer, 64, 1)
    outer = outer + pltpu.roll(outer, 32, 1)
    mixed = jnp.concatenate([jnp.sum(spread[k] * outer, axis=0, keepdims=True) for k in range(16)], axis=0)
    feat[...] = (mixed / count).astype(BF16)

    def copy2(d):
        return pltpu.make_async_remote_copy(
            feat, recv2.at[z], send2.at[d - 1], got2, device_id=at_z((z + d) % 16), device_id_type=MESH
        )

    for d in range(1, 16):
        copy2(d).start()
    recv2[z] = feat[...]
    pltpu.make_async_copy(recv2.at[pl.ds(0, 15)], recv2.at[pl.ds(0, 15)], got2).wait()
    ordered = jnp.dot(perm[...], recv2[...].reshape(256, 128), preferred_element_type=F32).astype(BF16)
    total_q = jnp.zeros((32, 256), F32)
    pltpu.make_async_copy(qall, qall, gotq).wait()
    for h in range(8):
        lhs = jnp.concatenate([ordered[64 * h : 64 * h + 32], ordered[64 * h + 32 : 64 * h + 64]], axis=1)
        total_q = total_q + lax.dot_general(lhs, qall[h], NT, preferred_element_type=F32)
    score[0] = total_q[:, :128]
    score[1] = total_q[:, 128:]

    def each3(act_on):
        for block in range(4):
            for group in range(4):
                to = (block // 2 * 32 + z * 2 + block % 2, ylo * 4 + group)
                mine = (ex == to[0]) & (hid == to[1])
                src = score.at[block // 2, pl.ds(8 * group, 8)]
                act_on(src, to, mine, 4 * block + group)

    slot = core * 8 + hid

    def start3(src, to, mine, index):
        @pl.when(mine)
        def _():
            pltpu.make_async_copy(src, recv3.at[slot], got3).start()

        @pl.when(jnp.logical_not(mine))
        def _():
            pltpu.make_async_remote_copy(
                src, recv3.at[slot], send3.at[index], got3, device_id=to, device_id_type=MESH
            ).start()

    each3(start3)
    pltpu.make_async_copy(recv3, recv3, got3).wait()
    for c in range(2):
        for k in range(4):
            block = recv3[8 * c + 2 * k] + recv3[8 * c + 2 * k + 1]
            for g in range(4):
                rows[8 * g + 4 * c + k : 8 * g + 4 * c + k + 1, :] = block[g : g + 1]
    done = rows[...]
    out[...] = jnp.where(core == 0, done, pltpu.roll(done, 64, 1))[:, :64]

    for d in range(1, 8):
        copy1(d).wait_send()
    for d in range(1, 32):
        copyq(d).wait_send()
    for d in range(1, 16):
        copy2(d).wait_send()

    def end3(src, to, mine, index):
        @pl.when(jnp.logical_not(mine))
        def _():
            pltpu.make_async_remote_copy(
                src, recv3.at[slot], send3.at[index], got3, device_id=to, device_id_type=MESH
            ).wait_send()

    each3(end3)


def local(activations, out_grads, token_mask, proj_in, proj_out, inv_input, inv_output, query_feats):
    hbm = pl.BlockSpec(memory_space=pl.ANY)
    result = pl.pallas_call(
        kernel,
        out_shape=jax.ShapeDtypeStruct((32, 64), F32),
        in_specs=[hbm] * 8,
        out_specs=pl.BlockSpec(memory_space=pltpu.VMEM),
        scratch_shapes=[
            pltpu.VMEM((4, 192, 1792), BF16),
            pltpu.VMEM((4, 192, 512), BF16),
            pltpu.VMEM((4, 192), jnp.int32),
            pltpu.VMEM((128, 1792), BF16),
            pltpu.VMEM((256, 512), BF16),
            pltpu.VMEM((64, 64), F32),
            pltpu.VMEM((64, 64), F32),
            pltpu.VMEM((64, 512), BF16),
            pltpu.VMEM((8, 144, 128), SEND),
            pltpu.VMEM((7, 144, 128), SEND),
            pltpu.VMEM((16, 64, 128), F32),
            pltpu.VMEM((2, 64, 256), BF16),
            pltpu.VMEM((8, 256, 256), BF16),
            pltpu.VMEM((512, 256), BF16),
            pltpu.VMEM((16, 128), BF16),
            pltpu.VMEM((16, 16, 128), BF16),
            pltpu.VMEM((2, 32, 128), F32),
            pltpu.VMEM((16, 8, 128), F32),
            pltpu.VMEM((32, 128), F32),
            pltpu.SemaphoreType.DMA((22,)),
        ]
        + [
            pltpu.SemaphoreType.DMA((7,)),
            pltpu.SemaphoreType.DMA,
            pltpu.SemaphoreType.DMA((31,)),
            pltpu.SemaphoreType.DMA,
            pltpu.SemaphoreType.DMA((15,)),
            pltpu.SemaphoreType.DMA,
            pltpu.SemaphoreType.DMA((16,)),
            pltpu.SemaphoreType.DMA,
        ],
        compiler_params=pltpu.CompilerParams(
            collective_id=0, has_side_effects=True, vmem_limit_bytes=40 << 20
        ),
        name="scores",
    )(
        activations,
        out_grads,
        token_mask,
        proj_in.T,
        proj_out.T,
        inv_input,
        inv_output,
        query_feats,
    )
    return result.T


def solution(mesh):
    return jax.shard_map(
        local,
        mesh=mesh,
        in_specs=(
            P("ex", None, "hid"),
            P("ex", None, "hid"),
            P("ex", None),
            P("hid", None),
            P("hid", None),
            P(),
            P(),
            P("ex", "hid"),
        ),
        out_specs=P("ex", "hid"),
        check_vma=False,
    )
```

```python
import functools

import jax
import jax.numpy as jnp
from jax import lax
from jax.experimental import pallas as pl
from jax.experimental.pallas import tpu as pltpu
from jax.sharding import PartitionSpec as P

MESH = pl.DeviceIdType.MESH
F32 = jnp.float32
BF16 = jnp.bfloat16
SEND = jnp.float32
NT = (((1,), (1,)), ((), ()))
TN = (((0,), (0,)), ((), ()))
HIGHEST = lax.Precision.HIGHEST


def iota(shape, dim):
    return lax.broadcasted_iota(jnp.int32, shape, dim)


def kernel(
    act, grads, mask, proj_in, proj_out, inv_in, inv_out, query, out,
    act_v, grads_v, mask_v, win_v, wout_v, invin_v, invout_v, query_v,
    part, recv1, spread, qsend, qall, perm, feat, recv2,
    in_sem, send1, got1, sendq, gotq, send2, got2, send3, got3, met1, met2,
):
    ex, hid = lax.axis_index("ex"), lax.axis_index("hid")
    ylo, z, core = ex // 32, (ex // 2) % 16, ex % 2
    x, yhi = hid // 2, hid % 2

    def near(dy, dz):
        return (((ylo + dy) % 2) * 32 + ((z + dz + 16) % 16) * 2 + core, hid)

    def tell(sem, to):
        pl.semaphore_signal(sem, inc=1, device_id=to, device_id_type=MESH)

    other = (ex + 1 - 2 * core, hid)

    copies = []

    def load(src, dst):
        copy = pltpu.make_async_copy(src, dst, in_sem.at[len(copies)])
        copy.start()
        copies.append(copy)
        return copy

    loads = [load(proj_in, win_v.at[pl.ds(64 * k, 64)]) for k in range(2)]
    for half in range(2):
        for group in range(4):
            loads.append(
                load(proj_out.at[pl.ds(32 * half, 32)], wout_v.at[pl.ds(128 * half + 32 * group, 32)])
            )
    stages = []
    for s in range(4):
        stages.append([load(act.at[s], act_v.at[s]), load(grads.at[s], grads_v.at[s])])
    late = [load(query, query_v), load(inv_in, invin_v), load(inv_out, invout_v), load(mask, mask_v)]

    barrier = pltpu.get_barrier_semaphore()
    for d in range(1, 8):
        tell(barrier, (ex, (hid + d) % 8))
    tell(barrier, other)
    tell(barrier, near(1, 0))
    for d in (-4, -3, -2, -1, 1, 2, 3, 4):
        tell(barrier, near(0, d))

    for copy in loads:
        copy.wait()
    lane48 = iota((48, 128), 1)
    lane96 = iota((96, 128), 1)
    for stage in ((0, 1), (2, 3)):
        for s in stage:
            for copy in stages[s]:
                copy.wait()
        for s in stage:
            y = lax.dot_general(act_v[s], win_v[...], NT, preferred_element_type=F32)
            packed = jnp.where(lane96 < 64, y[:96], y[96:]).astype(SEND)
            o = lax.dot_general(grads_v[s], wout_v[...], NT, preferred_element_type=F32)
            for half in range(2):
                c = o[:, 128 * half : 128 * half + 128]
                picked = jnp.where(
                    lane48 < 64,
                    jnp.where(lane48 < 32, c[:48], c[48:96]),
                    jnp.where(lane48 < 96, c[96:144], c[144:]),
                )
                part[2 * s + half, :96] = packed
                part[2 * s + half, 96:] = picked.astype(SEND)

    pl.semaphore_wait(barrier, 17)

    def copy1(d):
        to = (hid + d) % 8
        return pltpu.make_async_remote_copy(
            part.at[to], recv1.at[d - 1], send1.at[d - 1], got1, device_id=(ex, to), device_id_type=MESH
        )

    for d in range(1, 8):
        copy1(d).start()
    for d in (-4, -3, -2, -1, 1, 2, 3, 4):
        tell(met1, near(0, d))

    for copy in late:
        copy.wait()
    m, col = iota((64, 128), 0), iota((64, 128), 1)
    place = m == 32 * (col // 64) + col % 32
    even = jnp.where(place & ((col // 32) % 2 == 0), 1.0, 0.0).astype(F32)
    odd = jnp.where(place & ((col // 32) % 2 == 1), 1.0, 0.0).astype(F32)
    both = jnp.concatenate(
        [
            jnp.dot(invout_v[...], even, precision=HIGHEST, preferred_element_type=F32),
            jnp.dot(invout_v[...], odd, precision=HIGHEST, preferred_element_type=F32),
        ],
        axis=0,
    )
    pre = [
        jnp.dot(
            query_v[:, 128 * b : 128 * b + 128].astype(F32), both, precision=HIGHEST, preferred_element_type=F32
        )
        for b in range(4)
    ]
    lane64 = iota((64, 128), 1)
    for b in range(2):
        left, right = pre[2 * b], pre[2 * b + 1]
        qsend[:, 128 * b : 128 * b + 128] = jnp.where(lane64 < 64, left, pltpu.roll(right, 64, 1)).astype(BF16)
        qsend[:, 256 + 128 * b : 384 + 128 * b] = jnp.where(
            lane64 < 64, pltpu.roll(left, 64, 1), right
        ).astype(BF16)
    qall[hid] = qsend[...]

    def copyq(d):
        return pltpu.make_async_remote_copy(
            qsend, qall.at[hid], sendq.at[d - 1], gotq, device_id=(ex, (hid + d) % 8), device_id_type=MESH
        )

    pl.semaphore_wait(met1, 8)
    for dy in range(2):
        for dz in (-4, 4):
            tell(met2, near(dy, dz))

    i, f = iota((64, 128), 0), iota((64, 128), 1)
    for k in range(16):
        pick = jnp.where(i == 4 * k + f // 32, 1.0, 0.0).astype(F32)
        spread[k] = jnp.dot(invin_v[...], pick, precision=HIGHEST, preferred_element_type=F32)
    r, c = iota((256, 256), 0), iota((256, 256), 1)
    perm[...] = jnp.where((c % 16 == r // 16) & (c // 16 == r % 16), 1.0, 0.0).astype(BF16)
    mask_row = mask_v[pl.ds(x, 1), :].astype(F32)
    count = jnp.sum(mask_row, axis=1, keepdims=True)
    t0, t1 = iota((48, 192), 0), iota((48, 192), 1)
    chosen = jnp.where(t1 % 48 == t0, 1.0, 0.0).astype(F32) * mask_row
    u0, u1 = iota((192, 128), 0), iota((192, 128), 1)
    group_of = jnp.where(u0 // 48 == u1 // 32, 1.0, 0.0).astype(BF16)
    weight = jnp.dot(chosen.astype(BF16), group_of, preferred_element_type=F32)
    pl.semaphore_wait(met2, 4)

    pltpu.make_async_copy(recv1, recv1, got1).wait()
    total = part[hid].astype(F32)
    for d in range(7):
        total = total + recv1[d].astype(F32)
    side_in = total[:96]
    side_out = total[96:] * weight
    in_hi = side_in.astype(BF16)
    in_lo = (side_in - in_hi.astype(F32)).astype(BF16)
    out_hi = side_out.astype(BF16)
    out_lo = (side_out - out_hi.astype(F32)).astype(BF16)
    right = jnp.concatenate([out_hi, out_lo, out_hi], axis=0)
    first = lax.dot_general(
        jnp.concatenate([in_hi[:48], in_hi[:48], in_lo[:48]], axis=0), right, TN, preferred_element_type=F32
    )
    second = lax.dot_general(
        jnp.concatenate([in_hi[48:], in_hi[48:], in_lo[48:]], axis=0), right, TN, preferred_element_type=F32
    )
    outer = jnp.where(
        lane64 < 64,
        jnp.where(lane64 < 32, first[:64], second[:64]),
        jnp.where(lane64 < 96, first[64:], second[64:]),
    )
    outer = outer + pltpu.roll(outer, 64, 1)
    outer = outer + pltpu.roll(outer, 32, 1)
    mixed = jnp.concatenate([jnp.sum(spread[k] * outer, axis=0, keepdims=True) for k in range(16)], axis=0)
    feat[...] = (mixed / count).astype(BF16)

    home = ex // 8
    slot = (z % 4) * 4 + x
    order = [(dy, dz) for dz in (8, 7, 9, 6, 10, 5, 11, 4, 12, 3, 13, 2, 14, 1, 15, 0) for dy in (1, 0)]

    def copy2(n):
        return pltpu.make_async_remote_copy(
            feat, recv2.at[0, yhi, slot], send2.at[n], got2,
            device_id=(near(*order[n])[0], home), device_id_type=MESH,
        )

    for n in range(31):
        copy2(n).start()

    @pl.when(hid != home)
    def _():
        copy2(31).start()

    @pl.when(hid == home)
    def _():
        pltpu.make_async_copy(feat, recv2.at[0, yhi, slot], got2).start()

    for d in range(1, 8):
        copyq(d).start()

    for d in range(1, 8):
        copy1(d).wait_send()
    for n in range(31):
        copy2(n).wait_send()

    @pl.when(hid != home)
    def _():
        copy2(31).wait_send()

    for d in range(1, 8):
        copyq(d).wait_send()
    pltpu.make_async_copy(qall.at[pl.ds(0, 7)], qall.at[pl.ds(0, 7)], gotq).wait()
    pltpu.make_async_copy(recv2.at[0], recv2.at[0], got2).wait()

    copy3 = pltpu.make_async_remote_copy(
        recv2.at[0], recv2.at[1], send3, got3, device_id=other, device_id_type=MESH
    )
    copy3.start()
    queries = jnp.concatenate([qall[h] for h in range(8)], axis=1)

    def scores(side):
        ordered = [
            jnp.dot(perm[...], recv2[side, half].reshape(256, 128), preferred_element_type=F32).astype(BF16)
            for half in range(2)
        ]
        lhs = jnp.concatenate(
            [
                ordered[half][32 * h + 16 * k : 32 * h + 16 * k + 16]
                for h in range(8)
                for half in range(2)
                for k in range(2)
            ],
            axis=1,
        )
        return lax.dot_general(lhs, queries, NT, preferred_element_type=F32)

    mine = scores(0)
    copy3.wait()
    theirs = scores(1)
    even = jnp.where(core == 0, mine, theirs)
    odd = jnp.where(core == 0, theirs, mine)
    for g in range(4):
        out[8 * g : 8 * g + 4, :] = even[4 * g : 4 * g + 4]
        out[8 * g + 4 : 8 * g + 8, :] = odd[4 * g : 4 * g + 4]


def local(activations, out_grads, token_mask, proj_in, proj_out, inv_input, inv_output, query_feats):
    hbm = pl.BlockSpec(memory_space=pltpu.HBM)
    result = pl.pallas_call(
        kernel,
        out_shape=jax.ShapeDtypeStruct((32, 64), F32),
        in_specs=[hbm] * 8,
        out_specs=pl.BlockSpec(memory_space=pltpu.VMEM),
        scratch_shapes=[
            pltpu.VMEM((4, 192, 1792), BF16),
            pltpu.VMEM((4, 192, 512), BF16),
            pltpu.VMEM((4, 192), jnp.int32),
            pltpu.VMEM((128, 1792), BF16),
            pltpu.VMEM((256, 512), BF16),
            pltpu.VMEM((64, 64), F32),
            pltpu.VMEM((64, 64), F32),
            pltpu.VMEM((64, 512), BF16),
            pltpu.VMEM((8, 144, 128), SEND),
            pltpu.VMEM((7, 144, 128), SEND),
            pltpu.VMEM((16, 64, 128), F32),
            pltpu.VMEM((64, 512), BF16),
            pltpu.VMEM((8, 64, 512), BF16),
            pltpu.VMEM((256, 256), BF16),
            pltpu.VMEM((16, 128), BF16),
            pltpu.VMEM((2, 2, 16, 16, 128), BF16),
            pltpu.SemaphoreType.DMA((22,)),
            pltpu.SemaphoreType.DMA((7,)),
            pltpu.SemaphoreType.DMA,
            pltpu.SemaphoreType.DMA((7,)),
            pltpu.SemaphoreType.DMA,
            pltpu.SemaphoreType.DMA((32,)),
            pltpu.SemaphoreType.DMA,
            pltpu.SemaphoreType.DMA,
            pltpu.SemaphoreType.DMA,
            pltpu.SemaphoreType.REGULAR,
            pltpu.SemaphoreType.REGULAR,
        ],
        compiler_params=pltpu.CompilerParams(
            collective_id=0, has_side_effects=True, vmem_limit_bytes=66_000_000
        ),
        name="scores",
    )(
        activations,
        out_grads,
        token_mask,
        proj_in.T,
        proj_out.T,
        inv_input,
        inv_output,
        query_feats,
    )
    return result.T


def solution(mesh):
    return jax.shard_map(
        local,
        mesh=mesh,
        in_specs=(
            P("ex", None, "hid"),
            P("ex", None, "hid"),
            P("ex", None),
            P("hid", None),
            P("hid", None),
            P(),
            P(),
            P("ex", "hid"),
        ),
        out_specs=P("ex", "hid"),
        check_vma=False,
    )
```

```python
import functools

import jax
import jax.numpy as jnp
from jax import lax
from jax.experimental import pallas as pl
from jax.experimental.pallas import tpu as pltpu
from jax.sharding import PartitionSpec as P

MESH = pl.DeviceIdType.MESH
F32 = jnp.float32
BF16 = jnp.bfloat16
IN_SENT, OUT_SENT = BF16, F32
NT = (((1,), (1,)), ((), ()))
TN = (((0,), (0,)), ((), ()))
HIGHEST = lax.Precision.HIGHEST


def iota(shape, dim):
    return lax.broadcasted_iota(jnp.int32, shape, dim)


def kernel(
    act, grads, mask, proj_in, proj_out, inv_in, inv_out, query, out,
    act_v, grads_v, mask_v, win_v, wout_v, invin_v, invout_v, query_v,
    part_in, part_out, own_in, own_out, from_in, from_out, spread, qsend, qall, perm, feat, recv2,
    in_sem, send1_in, send1_out, got1_in, got1_out, sendq, gotq, send2, got2, send3, got3, met1, met2,
):
    ex, hid = lax.axis_index("ex"), lax.axis_index("hid")
    ylo, z, core = ex // 32, (ex // 2) % 16, ex % 2
    x, yhi = hid // 2, hid % 2

    def near(dy, dz):
        return (((ylo + dy) % 2) * 32 + ((z + dz + 16) % 16) * 2 + core, hid)

    def tell(sem, to):
        pl.semaphore_signal(sem, inc=1, device_id=to, device_id_type=MESH)

    other = (ex + 1 - 2 * core, hid)

    copies = []

    def load(src, dst):
        copy = pltpu.make_async_copy(src, dst, in_sem.at[len(copies)])
        copy.start()
        copies.append(copy)
        return copy

    def sequence(step):
        s = (x + step) % 4
        return [load(act.at[s], act_v.at[step]), load(grads.at[s], grads_v.at[step])]

    loads = [load(proj_in, win_v.at[pl.ds(64 * k, 64)]) for k in range(2)]
    first = sequence(2)
    for half in range(2):
        for group in range(4):
            loads.append(
                load(proj_out.at[pl.ds(32 * half, 32)], wout_v.at[pl.ds(128 * half + 32 * group, 32)])
            )

    barrier = pltpu.get_barrier_semaphore()
    for d in range(1, 8):
        tell(barrier, (ex, (hid + d) % 8))
    for d in (-4, -3, -2, -1, 1, 2, 3, 4):
        tell(barrier, near(0, d))
    tell(barrier, other)
    tell(barrier, near(1, 0))
    rest = [copy for step in (1, 3, 0) for copy in sequence(step)]
    late = [load(query, query_v), load(inv_in, invin_v), load(inv_out, invout_v), load(mask, mask_v)]

    lane48 = iota((48, 128), 1)
    lane96 = iota((96, 128), 1)

    def project(step):
        y = lax.dot_general(act_v[step], win_v[...], NT, preferred_element_type=F32)
        packed = jnp.where(lane96 < 64, y[:96], y[96:])
        part_in[step] = packed.astype(IN_SENT)
        o = lax.dot_general(grads_v[step], wout_v[...], NT, preferred_element_type=F32)
        if step == 0:
            own_in[...] = packed
        for half in range(2):
            c = o[:, 128 * half : 128 * half + 128]
            picked = jnp.where(
                lane48 < 64,
                jnp.where(lane48 < 32, c[:48], c[48:96]),
                jnp.where(lane48 < 96, c[96:144], c[144:]),
            )
            part_out[step, half] = picked.astype(OUT_SENT)
            if step == 0:
                own_out[half] = picked

    def copy1(n):
        step, half = ((2, 0), (2, 1), (1, 0), (1, 1), (3, 0), (3, 1), (0, 1 - yhi))[n]
        to = ((x + step) % 4) * 2 + half
        at = (to - hid + 8) % 8 - 1
        return [
            pltpu.make_async_remote_copy(
                part_in.at[step], from_in.at[at], send1_in.at[n], got1_in, device_id=(ex, to), device_id_type=MESH
            ),
            pltpu.make_async_remote_copy(
                part_out.at[step, half], from_out.at[at], send1_out.at[n], got1_out,
                device_id=(ex, to), device_id_type=MESH,
            ),
        ]

    def start1(messages):
        for n in messages:
            for copy in copy1(n):
                copy.start()

    for copy in loads + first:
        copy.wait()
    for copy in rest:
        copy.wait()
    for step in (2, 1, 3, 0):
        project(step)
    pl.semaphore_wait(barrier, 17)
    start1(range(7))
    for d in (-4, -3, -2, -1, 1, 2, 3, 4):
        tell(met1, near(0, d))

    for copy in late:
        copy.wait()
    m, col = iota((64, 128), 0), iota((64, 128), 1)
    place = m == 32 * (col // 64) + col % 32
    even = jnp.where(place & ((col // 32) % 2 == 0), 1.0, 0.0).astype(F32)
    odd = jnp.where(place & ((col // 32) % 2 == 1), 1.0, 0.0).astype(F32)
    both = jnp.concatenate(
        [
            jnp.dot(invout_v[...], even, precision=HIGHEST, preferred_element_type=F32),
            jnp.dot(invout_v[...], odd, precision=HIGHEST, preferred_element_type=F32),
        ],
        axis=0,
    )
    pre = [
        jnp.dot(
            query_v[:, 128 * b : 128 * b + 128].astype(F32), both, precision=HIGHEST, preferred_element_type=F32
        )
        for b in range(4)
    ]
    lane64 = iota((64, 128), 1)
    for b in range(2):
        left, right = pre[2 * b], pre[2 * b + 1]
        qsend[:, 128 * b : 128 * b + 128] = jnp.where(lane64 < 64, left, pltpu.roll(right, 64, 1)).astype(BF16)
        qsend[:, 256 + 128 * b : 384 + 128 * b] = jnp.where(
            lane64 < 64, pltpu.roll(left, 64, 1), right
        ).astype(BF16)
    qall[hid] = qsend[...]

    def copyq(d):
        return pltpu.make_async_remote_copy(
            qsend, qall.at[hid], sendq.at[d - 1], gotq, device_id=(ex, (hid + d) % 8), device_id_type=MESH
        )

    pl.semaphore_wait(met1, 8)
    for dy in range(2):
        for dz in (-4, 4):
            tell(met2, near(dy, dz))

    i, f = iota((64, 128), 0), iota((64, 128), 1)
    for k in range(16):
        pick = jnp.where(i == 4 * k + f // 32, 1.0, 0.0).astype(F32)
        spread[k] = jnp.dot(invin_v[...], pick, precision=HIGHEST, preferred_element_type=F32)
    r, c = iota((256, 256), 0), iota((256, 256), 1)
    perm[...] = jnp.where((c % 16 == r // 16) & (c // 16 == r % 16), 1.0, 0.0).astype(BF16)
    mask_row = mask_v[pl.ds(x, 1), :].astype(F32)
    count = jnp.sum(mask_row, axis=1, keepdims=True)
    t0, t1 = iota((48, 192), 0), iota((48, 192), 1)
    chosen = jnp.where(t1 % 48 == t0, 1.0, 0.0).astype(F32) * mask_row
    u0, u1 = iota((192, 128), 0), iota((192, 128), 1)
    group_of = jnp.where(u0 // 48 == u1 // 32, 1.0, 0.0).astype(BF16)
    weight = jnp.dot(chosen.astype(BF16), group_of, preferred_element_type=F32)
    pl.semaphore_wait(met2, 4)

    pltpu.make_async_copy(from_out, from_out, got1_out).wait()
    pltpu.make_async_copy(from_in, from_in, got1_in).wait()
    side_in, side_out = own_in[...], own_out[yhi]
    for n in range(7):
        side_in = side_in + from_in[n].astype(F32)
        side_out = side_out + from_out[n].astype(F32)
    side_out = side_out * weight
    in_hi = side_in.astype(BF16)
    in_lo = (side_in - in_hi.astype(F32)).astype(BF16)
    out_hi = side_out.astype(BF16)
    out_lo = (side_out - out_hi.astype(F32)).astype(BF16)
    right = jnp.concatenate([out_hi, out_lo, out_hi], axis=0)
    first = lax.dot_general(
        jnp.concatenate([in_hi[:48], in_hi[:48], in_lo[:48]], axis=0), right, TN, preferred_element_type=F32
    )
    second = lax.dot_general(
        jnp.concatenate([in_hi[48:], in_hi[48:], in_lo[48:]], axis=0), right, TN, preferred_element_type=F32
    )
    outer = jnp.where(
        lane64 < 64,
        jnp.where(lane64 < 32, first[:64], second[:64]),
        jnp.where(lane64 < 96, first[64:], second[64:]),
    )
    outer = outer + pltpu.roll(outer, 64, 1)
    outer = outer + pltpu.roll(outer, 32, 1)
    mixed = jnp.concatenate([jnp.sum(spread[k] * outer, axis=0, keepdims=True) for k in range(16)], axis=0)
    feat[...] = (mixed / count).astype(BF16)

    home = ex // 8
    slot = (z % 4) * 4 + x
    order = [(dy, dz) for dz in (8, 7, 9, 6, 10, 5, 11, 4, 12, 3, 13, 2, 14, 1, 15, 0) for dy in (1, 0)]

    def copy2(n):
        return pltpu.make_async_remote_copy(
            feat, recv2.at[0, yhi, slot], send2.at[n], got2,
            device_id=(near(*order[n])[0], home), device_id_type=MESH,
        )

    for n in range(31):
        copy2(n).start()

    @pl.when(hid != home)
    def _():
        copy2(31).start()

    @pl.when(hid == home)
    def _():
        pltpu.make_async_copy(feat, recv2.at[0, yhi, slot], got2).start()

    for d in range(1, 8):
        copyq(d).start()

    for n in range(7):
        for copy in copy1(n):
            copy.wait_send()
    for n in range(31):
        copy2(n).wait_send()

    @pl.when(hid != home)
    def _():
        copy2(31).wait_send()

    for d in range(1, 8):
        copyq(d).wait_send()
    pltpu.make_async_copy(qall.at[pl.ds(0, 7)], qall.at[pl.ds(0, 7)], gotq).wait()
    pltpu.make_async_copy(recv2.at[0], recv2.at[0], got2).wait()

    copy3 = pltpu.make_async_remote_copy(
        recv2.at[0], recv2.at[1], send3, got3, device_id=other, device_id_type=MESH
    )
    copy3.start()
    queries = jnp.concatenate([qall[h] for h in range(8)], axis=1)

    def scores(side):
        ordered = [
            jnp.dot(perm[...], recv2[side, half].reshape(256, 128), preferred_element_type=F32).astype(BF16)
            for half in range(2)
        ]
        lhs = jnp.concatenate(
            [
                ordered[half][32 * h + 16 * k : 32 * h + 16 * k + 16]
                for h in range(8)
                for half in range(2)
                for k in range(2)
            ],
            axis=1,
        )
        return lax.dot_general(lhs, queries, NT, preferred_element_type=F32)

    mine = scores(0)
    copy3.wait()
    theirs = scores(1)
    even = jnp.where(core == 0, mine, theirs)
    odd = jnp.where(core == 0, theirs, mine)
    for g in range(4):
        out[8 * g : 8 * g + 4, :] = even[4 * g : 4 * g + 4]
        out[8 * g + 4 : 8 * g + 8, :] = odd[4 * g : 4 * g + 4]


def local(activations, out_grads, token_mask, proj_in, proj_out, inv_input, inv_output, query_feats):
    hbm = pl.BlockSpec(memory_space=pltpu.HBM)
    result = pl.pallas_call(
        kernel,
        out_shape=jax.ShapeDtypeStruct((32, 64), F32),
        in_specs=[hbm] * 8,
        out_specs=pl.BlockSpec(memory_space=pltpu.VMEM),
        scratch_shapes=[
            pltpu.VMEM((4, 192, 1792), BF16),
            pltpu.VMEM((4, 192, 512), BF16),
            pltpu.VMEM((4, 192), jnp.int32),
            pltpu.VMEM((128, 1792), BF16),
            pltpu.VMEM((256, 512), BF16),
            pltpu.VMEM((64, 64), F32),
            pltpu.VMEM((64, 64), F32),
            pltpu.VMEM((64, 512), BF16),
            pltpu.VMEM((4, 96, 128), IN_SENT),
            pltpu.VMEM((4, 2, 48, 128), OUT_SENT),
            pltpu.VMEM((96, 128), F32),
            pltpu.VMEM((2, 48, 128), F32),
            pltpu.VMEM((7, 96, 128), IN_SENT),
            pltpu.VMEM((7, 48, 128), OUT_SENT),
            pltpu.VMEM((16, 64, 128), F32),
            pltpu.VMEM((64, 512), BF16),
            pltpu.VMEM((8, 64, 512), BF16),
            pltpu.VMEM((256, 256), BF16),
            pltpu.VMEM((16, 128), BF16),
            pltpu.VMEM((2, 2, 16, 16, 128), BF16),
            pltpu.SemaphoreType.DMA((22,)),
            pltpu.SemaphoreType.DMA((7,)),
            pltpu.SemaphoreType.DMA((7,)),
            pltpu.SemaphoreType.DMA,
            pltpu.SemaphoreType.DMA,
            pltpu.SemaphoreType.DMA((7,)),
            pltpu.SemaphoreType.DMA,
            pltpu.SemaphoreType.DMA((32,)),
            pltpu.SemaphoreType.DMA,
            pltpu.SemaphoreType.DMA,
            pltpu.SemaphoreType.DMA,
            pltpu.SemaphoreType.REGULAR,
            pltpu.SemaphoreType.REGULAR,
        ],
        compiler_params=pltpu.CompilerParams(
            collective_id=0, has_side_effects=True, vmem_limit_bytes=40 << 20
        ),
        name="scores",
    )(
        *(
            pltpu.with_memory_space_constraint(array, pltpu.HBM)
            for array in (
                activations,
                out_grads,
                token_mask,
                proj_in.T,
                proj_out.T,
                inv_input,
                inv_output,
                query_feats,
            )
        )
    )
    return result.T


def solution(mesh):
    return jax.shard_map(
        local,
        mesh=mesh,
        in_specs=(
            P("ex", None, "hid"),
            P("ex", None, "hid"),
            P("ex", None),
            P("hid", None),
            P("hid", None),
            P(),
            P(),
            P("ex", "hid"),
        ),
        out_specs=P("ex", "hid"),
        check_vma=False,
    )
```

```python
import functools

import jax
import jax.numpy as jnp
from jax import lax
from jax.experimental import pallas as pl
from jax.experimental.pallas import tpu as pltpu
from jax.sharding import PartitionSpec as P

MESH = pl.DeviceIdType.MESH
F32 = jnp.float32
BF16 = jnp.bfloat16
IN_SENT, OUT_SENT = BF16, F32
NT = (((1,), (1,)), ((), ()))
TN = (((0,), (0,)), ((), ()))
HIGHEST = lax.Precision.HIGHEST


def iota(shape, dim):
    return lax.broadcasted_iota(jnp.int32, shape, dim)


def kernel(
    act, grads, mask, proj_in, proj_out, inv_in, inv_out, query, out,
    act_v, grads_v, mask_v, win_v, wout_v, invin_v, invout_v, query_v,
    part_in, part_out, own_in, own_out, from_in, from_out, spread, qsend, qall, perm, feat, recv2,
    in_sem, send1_in, send1_out, got1_in, got1_out, sendq, gotq, send2, got2, send3, got3, met1, met2,
):
    ex, hid = lax.axis_index("ex"), lax.axis_index("hid")
    ylo, z, core = ex // 32, (ex // 2) % 16, ex % 2
    x, yhi = hid // 2, hid % 2

    def near(dy, dz):
        return (((ylo + dy) % 2) * 32 + ((z + dz + 16) % 16) * 2 + core, hid)

    def tell(sem, to):
        pl.semaphore_signal(sem, inc=1, device_id=to, device_id_type=MESH)

    other = (ex + 1 - 2 * core, hid)

    copies = []

    def load(src, dst):
        copy = pltpu.make_async_copy(src, dst, in_sem.at[len(copies)])
        copy.start()
        copies.append(copy)
        return copy

    def sequence(step):
        s = (x + step) % 4
        return [load(act.at[s], act_v.at[step]), load(grads.at[s], grads_v.at[step])]

    late = [load(inv_in, invin_v), load(inv_out, invout_v), load(query, query_v), load(mask, mask_v)]
    first = [copy for step in (2, 1) for copy in sequence(step)]
    loads = [load(proj_in, win_v), load(proj_out, wout_v)]
    rest = [copy for step in (3, 0) for copy in sequence(step)]

    barrier = pltpu.get_barrier_semaphore()
    for d in range(1, 8):
        tell(barrier, (ex, (hid + d) % 8))
    for d in (-4, -3, -2, -1, 1, 2, 3, 4):
        tell(barrier, near(0, d))
    tell(barrier, other)
    tell(barrier, near(1, 0))
    lane48 = iota((48, 128), 1)
    lane96 = iota((96, 128), 1)

    def project(step):
        win = jnp.concatenate([win_v[...]] * 2, axis=0)
        wout = jnp.concatenate([wout_v[:32]] * 4 + [wout_v[32:]] * 4, axis=0)
        y = lax.dot_general(act_v[step], win, NT, preferred_element_type=F32)
        packed = jnp.where(lane96 < 64, y[:96], y[96:])
        part_in[step] = packed.astype(IN_SENT)
        o = lax.dot_general(grads_v[step], wout, NT, preferred_element_type=F32)
        if step == 0:
            own_in[...] = packed
        for half in range(2):
            c = o[:, 128 * half : 128 * half + 128]
            picked = jnp.where(
                lane48 < 64,
                jnp.where(lane48 < 32, c[:48], c[48:96]),
                jnp.where(lane48 < 96, c[96:144], c[144:]),
            )
            part_out[step, half] = picked.astype(OUT_SENT)
            if step == 0:
                own_out[half] = picked

    def copy1(n):
        step, half = ((2, 0), (2, 1), (1, 0), (1, 1), (3, 0), (3, 1), (0, 1 - yhi))[n]
        to = ((x + step) % 4) * 2 + half
        at = (to - hid + 8) % 8 - 1
        return [
            pltpu.make_async_remote_copy(
                part_in.at[step], from_in.at[at], send1_in.at[n], got1_in, device_id=(ex, to), device_id_type=MESH
            ),
            pltpu.make_async_remote_copy(
                part_out.at[step, half], from_out.at[at], send1_out.at[n], got1_out,
                device_id=(ex, to), device_id_type=MESH,
            ),
        ]

    def start1(messages):
        for n in messages:
            for copy in copy1(n):
                copy.start()

    for copy in loads + first:
        copy.wait()
    for step in (2, 1):
        project(step)
    pl.semaphore_wait(barrier, 17)
    start1((0, 1, 2, 3))
    for d in (-4, -3, -2, -1, 1, 2, 3, 4):
        tell(met1, near(0, d))
    for copy in rest:
        copy.wait()
    for step in (3, 0):
        project(step)
    start1((4, 5, 6))

    def exact3(array):
        high = array.astype(BF16)
        left = array - high.astype(F32)
        middle = left.astype(BF16)
        return high, middle, (left - middle.astype(F32)).astype(BF16)

    for copy in late:
        copy.wait()
    m, col = iota((64, 128), 0), iota((64, 128), 1)
    place = m == 32 * (col // 64) + col % 32
    even = jnp.where(place & ((col // 32) % 2 == 0), 1.0, 0.0).astype(BF16)
    odd = jnp.where(place & ((col // 32) % 2 == 1), 1.0, 0.0).astype(BF16)
    both = jnp.concatenate(
        [
            jnp.dot(piece, where_to, preferred_element_type=F32).astype(BF16)
            for piece in exact3(invout_v[...])
            for where_to in (even, odd)
        ],
        axis=0,
    )
    pre = [
        jnp.dot(
            jnp.concatenate([query_v[:, 128 * b : 128 * b + 128]] * 3, axis=1), both, preferred_element_type=F32
        )
        for b in range(4)
    ]
    lane64 = iota((64, 128), 1)
    for b in range(2):
        left, right = pre[2 * b], pre[2 * b + 1]
        qsend[:, 128 * b : 128 * b + 128] = jnp.where(lane64 < 64, left, pltpu.roll(right, 64, 1)).astype(BF16)
        qsend[:, 256 + 128 * b : 384 + 128 * b] = jnp.where(
            lane64 < 64, pltpu.roll(left, 64, 1), right
        ).astype(BF16)
    qall[hid] = qsend[...]

    pl.semaphore_wait(met1, 8)
    for dy in range(2):
        for dz in (-4, 4):
            tell(met2, near(dy, dz))

    i, f = iota((64, 128), 0), iota((64, 128), 1)
    pieces = jnp.concatenate(exact3(invin_v[...]), axis=1)
    for k in range(16):
        pick = jnp.where(i == 4 * k + f // 32, 1.0, 0.0).astype(BF16)
        spread[k] = jnp.dot(pieces, jnp.concatenate([pick] * 3, axis=0), preferred_element_type=F32)
    r, c = iota((256, 256), 0), iota((256, 256), 1)
    perm[...] = jnp.where((c % 16 == r // 16) & (c // 16 == r % 16), 1.0, 0.0).astype(BF16)
    mask_row = mask_v[pl.ds(x, 1), :].astype(F32)
    count = jnp.sum(mask_row, axis=1, keepdims=True)
    t0, t1 = iota((48, 192), 0), iota((48, 192), 1)
    chosen = jnp.where(t1 % 48 == t0, 1.0, 0.0).astype(F32) * mask_row
    u0, u1 = iota((192, 128), 0), iota((192, 128), 1)
    group_of = jnp.where(u0 // 48 == u1 // 32, 1.0, 0.0).astype(BF16)
    weight = jnp.dot(chosen.astype(BF16), group_of, preferred_element_type=F32)

    def copyq(d):
        return pltpu.make_async_remote_copy(
            qsend, qall.at[hid], sendq.at[d - 1], gotq, device_id=(ex, (hid + d) % 8), device_id_type=MESH
        )

    pl.semaphore_wait(met2, 4)

    pltpu.make_async_copy(from_out, from_out, got1_out).wait()
    pltpu.make_async_copy(from_in, from_in, got1_in).wait()
    side_in, side_out = own_in[...], own_out[yhi]
    for n in range(7):
        side_in = side_in + from_in[n].astype(F32)
        side_out = side_out + from_out[n].astype(F32)
    side_out = side_out * weight
    in_hi = side_in.astype(BF16)
    in_lo = (side_in - in_hi.astype(F32)).astype(BF16)
    out_hi = side_out.astype(BF16)
    out_lo = (side_out - out_hi.astype(F32)).astype(BF16)
    right = jnp.concatenate([out_hi, out_lo, out_hi], axis=0)
    first = lax.dot_general(
        jnp.concatenate([in_hi[:48], in_hi[:48], in_lo[:48]], axis=0), right, TN, preferred_element_type=F32
    )
    second = lax.dot_general(
        jnp.concatenate([in_hi[48:], in_hi[48:], in_lo[48:]], axis=0), right, TN, preferred_element_type=F32
    )
    outer = jnp.where(
        lane64 < 64,
        jnp.where(lane64 < 32, first[:64], second[:64]),
        jnp.where(lane64 < 96, first[64:], second[64:]),
    )
    outer = outer + pltpu.roll(outer, 64, 1)
    outer = outer + pltpu.roll(outer, 32, 1)
    mixed = jnp.concatenate([jnp.sum(spread[k] * outer, axis=0, keepdims=True) for k in range(16)], axis=0)
    feat[...] = (mixed / count).astype(BF16)

    home = ex // 8
    slot = (z % 4) * 4 + x
    order = [(dy, dz) for dz in (8, 7, 9, 6, 10, 5, 11, 4, 12, 3, 13, 2, 14, 1, 15, 0) for dy in (1, 0)]

    def copy2(n):
        return pltpu.make_async_remote_copy(
            feat, recv2.at[0, yhi, slot], send2.at[n], got2,
            device_id=(near(*order[n])[0], home), device_id_type=MESH,
        )

    for n in range(31):
        copy2(n).start()

    @pl.when(hid != home)
    def _():
        copy2(31).start()

    @pl.when(hid == home)
    def _():
        pltpu.make_async_copy(feat, recv2.at[0, yhi, slot], got2).start()

    for d in range(1, 8):
        copyq(d).start()

    for n in range(7):
        for copy in copy1(n):
            copy.wait_send()
    for n in range(31):
        copy2(n).wait_send()

    @pl.when(hid != home)
    def _():
        copy2(31).wait_send()

    for d in range(1, 8):
        copyq(d).wait_send()
    pltpu.make_async_copy(qall.at[pl.ds(0, 7)], qall.at[pl.ds(0, 7)], gotq).wait()
    pltpu.make_async_copy(recv2.at[0], recv2.at[0], got2).wait()

    copy3 = pltpu.make_async_remote_copy(
        recv2.at[0], recv2.at[1], send3, got3, device_id=other, device_id_type=MESH
    )
    copy3.start()
    queries = jnp.concatenate([qall[h] for h in range(8)], axis=1)

    def scores(side):
        ordered = [
            jnp.dot(perm[...], recv2[side, half].reshape(256, 128), preferred_element_type=F32).astype(BF16)
            for half in range(2)
        ]
        lhs = jnp.concatenate(
            [
                ordered[half][32 * h + 16 * k : 32 * h + 16 * k + 16]
                for h in range(8)
                for half in range(2)
                for k in range(2)
            ],
            axis=1,
        )
        return lax.dot_general(lhs, queries, NT, preferred_element_type=F32)

    mine = scores(0)
    copy3.wait()
    theirs = scores(1)
    even = jnp.where(core == 0, mine, theirs)
    odd = jnp.where(core == 0, theirs, mine)
    for g in range(4):
        out[8 * g : 8 * g + 4, :] = even[4 * g : 4 * g + 4]
        out[8 * g + 4 : 8 * g + 8, :] = odd[4 * g : 4 * g + 4]


def local(activations, out_grads, token_mask, proj_in, proj_out, inv_input, inv_output, query_feats):
    hbm = pl.BlockSpec(memory_space=pltpu.HBM)
    result = pl.pallas_call(
        kernel,
        out_shape=jax.ShapeDtypeStruct((32, 64), F32),
        in_specs=[hbm] * 8,
        out_specs=pl.BlockSpec(memory_space=pltpu.VMEM),
        scratch_shapes=[
            pltpu.VMEM((4, 192, 1792), BF16),
            pltpu.VMEM((4, 192, 512), BF16),
            pltpu.VMEM((4, 192), jnp.int32),
            pltpu.VMEM((64, 1792), BF16),
            pltpu.VMEM((64, 512), BF16),
            pltpu.VMEM((64, 64), F32),
            pltpu.VMEM((64, 64), F32),
            pltpu.VMEM((64, 512), BF16),
            pltpu.VMEM((4, 96, 128), IN_SENT),
            pltpu.VMEM((4, 2, 48, 128), OUT_SENT),
            pltpu.VMEM((96, 128), F32),
            pltpu.VMEM((2, 48, 128), F32),
            pltpu.VMEM((7, 96, 128), IN_SENT),
            pltpu.VMEM((7, 48, 128), OUT_SENT),
            pltpu.VMEM((16, 64, 128), F32),
            pltpu.VMEM((64, 512), BF16),
            pltpu.VMEM((8, 64, 512), BF16),
            pltpu.VMEM((256, 256), BF16),
            pltpu.VMEM((16, 128), BF16),
            pltpu.VMEM((2, 2, 16, 16, 128), BF16),
            pltpu.SemaphoreType.DMA((14,)),
            pltpu.SemaphoreType.DMA((7,)),
            pltpu.SemaphoreType.DMA((7,)),
            pltpu.SemaphoreType.DMA,
            pltpu.SemaphoreType.DMA,
            pltpu.SemaphoreType.DMA((7,)),
            pltpu.SemaphoreType.DMA,
            pltpu.SemaphoreType.DMA((32,)),
            pltpu.SemaphoreType.DMA,
            pltpu.SemaphoreType.DMA,
            pltpu.SemaphoreType.DMA,
            pltpu.SemaphoreType.REGULAR,
            pltpu.SemaphoreType.REGULAR,
        ],
        compiler_params=pltpu.CompilerParams(
            collective_id=0, has_side_effects=True, vmem_limit_bytes=40 << 20
        ),
        name="scores",
    )(
        *(
            pltpu.with_memory_space_constraint(array, pltpu.HBM)
            for array in (
                activations,
                out_grads,
                token_mask,
                proj_in.T,
                proj_out.T,
                inv_input,
                inv_output,
                query_feats,
            )
        )
    )
    return result.T


def solution(mesh):
    return jax.shard_map(
        local,
        mesh=mesh,
        in_specs=(
            P("ex", None, "hid"),
            P("ex", None, "hid"),
            P("ex", None),
            P("hid", None),
            P("hid", None),
            P(),
            P(),
            P("ex", "hid"),
        ),
        out_specs=P("ex", "hid"),
        check_vma=False,
    )
```

```python
import functools

import jax
import jax.numpy as jnp
from jax import lax
from jax.experimental import pallas as pl
from jax.experimental.pallas import tpu as pltpu
from jax.sharding import PartitionSpec as P

MESH = pl.DeviceIdType.MESH
F32 = jnp.float32
BF16 = jnp.bfloat16
IN_SENT, OUT_SENT = BF16, BF16
NT = (((1,), (1,)), ((), ()))
TN = (((0,), (0,)), ((), ()))
HIGHEST = lax.Precision.HIGHEST


def iota(shape, dim):
    return lax.broadcasted_iota(jnp.int32, shape, dim)


def kernel(
    act, grads, mask, proj_in, proj_out, inv_in, inv_out, query, out,
    act_v, grads_v, mask_v, win_v, wout_v, invin_v, invout_v, query_v,
    part_in, part_out, own_in, own_out, from_in, from_out, spread, qsend, qall, perm, feat, recv2,
    in_sem, send1_in, send1_out, got1_in, got1_out, sendq, gotq, send2, got2, send3, got3, met1, met2,
):
    ex, hid = lax.axis_index("ex"), lax.axis_index("hid")
    ylo, z, core = ex // 32, (ex // 2) % 16, ex % 2
    x, yhi = hid // 2, hid % 2

    def near(dy, dz):
        return (((ylo + dy) % 2) * 32 + ((z + dz + 16) % 16) * 2 + core, hid)

    def tell(sem, to):
        pl.semaphore_signal(sem, inc=1, device_id=to, device_id_type=MESH)

    other = (ex + 1 - 2 * core, hid)

    copies = []

    def load(src, dst):
        copy = pltpu.make_async_copy(src, dst, in_sem.at[len(copies)])
        copy.start()
        copies.append(copy)
        return copy

    def sequence(step):
        s = (x + step) % 4
        return [load(act.at[s], act_v.at[step]), load(grads.at[s], grads_v.at[step])]

    late = [load(inv_in, invin_v), load(inv_out, invout_v), load(query, query_v), load(mask, mask_v)]
    first = [copy for step in (2, 1) for copy in sequence(step)]
    loads = [load(proj_in, win_v), load(proj_out, wout_v)]
    rest = [copy for step in (3, 0) for copy in sequence(step)]

    barrier = pltpu.get_barrier_semaphore()
    for d in range(1, 8):
        tell(barrier, (ex, (hid + d) % 8))
    for d in (-4, -3, -2, -1, 1, 2, 3, 4):
        tell(barrier, near(0, d))
    tell(barrier, other)
    tell(barrier, near(1, 0))
    lane48 = iota((48, 128), 1)
    lane96 = iota((96, 128), 1)

    def project(step):
        win = jnp.concatenate([win_v[...]] * 2, axis=0)
        wout = jnp.concatenate([wout_v[:32]] * 4 + [wout_v[32:]] * 4, axis=0)
        y = lax.dot_general(act_v[step], win, NT, preferred_element_type=F32)
        packed = jnp.where(lane96 < 64, y[:96], y[96:])
        part_in[step] = packed.astype(IN_SENT)
        o = lax.dot_general(grads_v[step], wout, NT, preferred_element_type=F32)
        if step == 0:
            own_in[...] = packed
        for half in range(2):
            c = o[:, 128 * half : 128 * half + 128]
            picked = jnp.where(
                lane48 < 64,
                jnp.where(lane48 < 32, c[:48], c[48:96]),
                jnp.where(lane48 < 96, c[96:144], c[144:]),
            )
            part_out[step, half] = picked.astype(OUT_SENT)
            if step == 0:
                own_out[half] = picked

    def copy1(n):
        step, half = ((2, 0), (2, 1), (1, 0), (1, 1), (3, 0), (3, 1), (0, 1 - yhi))[n]
        to = ((x + step) % 4) * 2 + half
        at = (to - hid + 8) % 8 - 1
        return [
            pltpu.make_async_remote_copy(
                part_in.at[step], from_in.at[at], send1_in.at[n], got1_in, device_id=(ex, to), device_id_type=MESH
            ),
            pltpu.make_async_remote_copy(
                part_out.at[step, half], from_out.at[at], send1_out.at[n], got1_out,
                device_id=(ex, to), device_id_type=MESH,
            ),
        ]

    def start1(messages):
        for n in messages:
            for copy in copy1(n):
                copy.start()

    for copy in loads + first:
        copy.wait()
    for step in (2, 1):
        project(step)
    pl.semaphore_wait(barrier, 17)
    start1((0, 1, 2, 3))
    for d in (-4, -3, -2, -1, 1, 2, 3, 4):
        tell(met1, near(0, d))
    for copy in rest:
        copy.wait()
    for step in (3, 0):
        project(step)
    start1((4, 5, 6))

    def exact3(array):
        high = array.astype(BF16)
        left = array - high.astype(F32)
        middle = left.astype(BF16)
        return high, middle, (left - middle.astype(F32)).astype(BF16)

    for copy in late:
        copy.wait()
    m, col = iota((64, 128), 0), iota((64, 128), 1)
    place = m == 32 * (col // 64) + col % 32
    even = jnp.where(place & ((col // 32) % 2 == 0), 1.0, 0.0).astype(BF16)
    odd = jnp.where(place & ((col // 32) % 2 == 1), 1.0, 0.0).astype(BF16)
    both = jnp.concatenate(
        [
            jnp.dot(piece, where_to, preferred_element_type=F32).astype(BF16)
            for piece in exact3(invout_v[...])
            for where_to in (even, odd)
        ],
        axis=0,
    )
    pre = [
        jnp.dot(
            jnp.concatenate([query_v[:, 128 * b : 128 * b + 128]] * 3, axis=1), both, preferred_element_type=F32
        )
        for b in range(4)
    ]
    lane64 = iota((64, 128), 1)
    for b in range(2):
        left, right = pre[2 * b], pre[2 * b + 1]
        qsend[:, 128 * b : 128 * b + 128] = jnp.where(lane64 < 64, left, pltpu.roll(right, 64, 1)).astype(BF16)
        qsend[:, 256 + 128 * b : 384 + 128 * b] = jnp.where(
            lane64 < 64, pltpu.roll(left, 64, 1), right
        ).astype(BF16)
    qall[hid] = qsend[...]

    pl.semaphore_wait(met1, 8)
    for dy in range(2):
        for dz in (-4, 4):
            tell(met2, near(dy, dz))

    i, f = iota((64, 128), 0), iota((64, 128), 1)
    pieces = jnp.concatenate(exact3(invin_v[...]), axis=1)
    for k in range(16):
        pick = jnp.where(i == 4 * k + f // 32, 1.0, 0.0).astype(BF16)
        spread[k] = jnp.dot(pieces, jnp.concatenate([pick] * 3, axis=0), preferred_element_type=F32)
    r, c = iota((256, 256), 0), iota((256, 256), 1)
    perm[...] = jnp.where((c % 16 == r // 16) & (c // 16 == r % 16), 1.0, 0.0).astype(BF16)
    mask_row = mask_v[pl.ds(x, 1), :].astype(F32)
    count = jnp.sum(mask_row, axis=1, keepdims=True)
    t0, t1 = iota((48, 192), 0), iota((48, 192), 1)
    chosen = jnp.where(t1 % 48 == t0, 1.0, 0.0).astype(F32) * mask_row
    u0, u1 = iota((192, 128), 0), iota((192, 128), 1)
    group_of = jnp.where(u0 // 48 == u1 // 32, 1.0, 0.0).astype(BF16)
    weight = jnp.dot(chosen.astype(BF16), group_of, preferred_element_type=F32)

    def copyq(d):
        return pltpu.make_async_remote_copy(
            qsend, qall.at[hid], sendq.at[d - 1], gotq, device_id=(ex, (hid + d) % 8), device_id_type=MESH
        )


    pltpu.make_async_copy(from_out, from_out, got1_out).wait()
    pltpu.make_async_copy(from_in, from_in, got1_in).wait()
    side_in, side_out = own_in[...], own_out[yhi]
    for n in range(7):
        side_in = side_in + from_in[n].astype(F32)
        side_out = side_out + from_out[n].astype(F32)
    side_out = side_out * weight
    in_hi = side_in.astype(BF16)
    in_lo = (side_in - in_hi.astype(F32)).astype(BF16)
    out_hi = side_out.astype(BF16)
    out_lo = (side_out - out_hi.astype(F32)).astype(BF16)
    right = jnp.concatenate([out_hi, out_lo, out_hi], axis=0)
    first = lax.dot_general(
        jnp.concatenate([in_hi[:48], in_hi[:48], in_lo[:48]], axis=0), right, TN, preferred_element_type=F32
    )
    second = lax.dot_general(
        jnp.concatenate([in_hi[48:], in_hi[48:], in_lo[48:]], axis=0), right, TN, preferred_element_type=F32
    )
    outer = jnp.where(
        lane64 < 64,
        jnp.where(lane64 < 32, first[:64], second[:64]),
        jnp.where(lane64 < 96, first[64:], second[64:]),
    )
    outer = outer + pltpu.roll(outer, 64, 1)
    outer = outer + pltpu.roll(outer, 32, 1)
    mixed = jnp.concatenate([jnp.sum(spread[k] * outer, axis=0, keepdims=True) for k in range(16)], axis=0)
    feat[...] = (mixed / count).astype(BF16)

    home = ex // 8
    slot = (z % 4) * 4 + x
    early = [(0, dz) for dz in (4, 12, 3, 13, 2, 14, 1, 15)]
    order = early + [(dy, dz) for dz in (8, 7, 9, 6, 10, 5, 11, 4, 12, 3, 13, 2, 14, 1, 15, 0) for dy in (1, 0) if (dy, dz) not in early and (dy, dz) != (0, 0)] + [(0, 0)]

    def copy2(n):
        return pltpu.make_async_remote_copy(
            feat, recv2.at[0, yhi, slot], send2.at[n], got2,
            device_id=(near(*order[n])[0], home), device_id_type=MESH,
        )

    for n in range(len(early)):
        copy2(n).start()
    pl.semaphore_wait(met2, 4)
    for n in range(len(early), 31):
        copy2(n).start()

    @pl.when(hid != home)
    def _():
        copy2(31).start()

    @pl.when(hid == home)
    def _():
        pltpu.make_async_copy(feat, recv2.at[0, yhi, slot], got2).start()

    for d in range(1, 8):
        copyq(d).start()

    for n in range(7):
        for copy in copy1(n):
            copy.wait_send()
    for n in range(31):
        copy2(n).wait_send()

    @pl.when(hid != home)
    def _():
        copy2(31).wait_send()

    for d in range(1, 8):
        copyq(d).wait_send()
    pltpu.make_async_copy(qall.at[pl.ds(0, 7)], qall.at[pl.ds(0, 7)], gotq).wait()
    pltpu.make_async_copy(recv2.at[0], recv2.at[0], got2).wait()

    copy3 = pltpu.make_async_remote_copy(
        recv2.at[0], recv2.at[1], send3, got3, device_id=other, device_id_type=MESH
    )
    copy3.start()
    queries = jnp.concatenate([qall[h] for h in range(8)], axis=1)

    def scores(side):
        ordered = [
            jnp.dot(perm[...], recv2[side, half].reshape(256, 128), preferred_element_type=F32).astype(BF16)
            for half in range(2)
        ]
        lhs = jnp.concatenate(
            [
                ordered[half][32 * h + 16 * k : 32 * h + 16 * k + 16]
                for h in range(8)
                for half in range(2)
                for k in range(2)
            ],
            axis=1,
        )
        return lax.dot_general(lhs, queries, NT, preferred_element_type=F32)

    mine = scores(0)
    copy3.wait()
    theirs = scores(1)
    even = jnp.where(core == 0, mine, theirs)
    odd = jnp.where(core == 0, theirs, mine)
    for g in range(4):
        out[8 * g : 8 * g + 4, :] = even[4 * g : 4 * g + 4]
        out[8 * g + 4 : 8 * g + 8, :] = odd[4 * g : 4 * g + 4]


def local(activations, out_grads, token_mask, proj_in, proj_out, inv_input, inv_output, query_feats):
    hbm = pl.BlockSpec(memory_space=pltpu.HBM)
    result = pl.pallas_call(
        kernel,
        out_shape=jax.ShapeDtypeStruct((32, 64), F32),
        in_specs=[hbm] * 8,
        out_specs=pl.BlockSpec(memory_space=pltpu.VMEM),
        scratch_shapes=[
            pltpu.VMEM((4, 192, 1792), BF16),
            pltpu.VMEM((4, 192, 512), BF16),
            pltpu.VMEM((4, 192), jnp.int32),
            pltpu.VMEM((64, 1792), BF16),
            pltpu.VMEM((64, 512), BF16),
            pltpu.VMEM((64, 64), F32),
            pltpu.VMEM((64, 64), F32),
            pltpu.VMEM((64, 512), BF16),
            pltpu.VMEM((4, 96, 128), IN_SENT),
            pltpu.VMEM((4, 2, 48, 128), OUT_SENT),
            pltpu.VMEM((96, 128), F32),
            pltpu.VMEM((2, 48, 128), F32),
            pltpu.VMEM((7, 96, 128), IN_SENT),
            pltpu.VMEM((7, 48, 128), OUT_SENT),
            pltpu.VMEM((16, 64, 128), F32),
            pltpu.VMEM((64, 512), BF16),
            pltpu.VMEM((8, 64, 512), BF16),
            pltpu.VMEM((256, 256), BF16),
            pltpu.VMEM((16, 128), BF16),
            pltpu.VMEM((2, 2, 16, 16, 128), BF16),
            pltpu.SemaphoreType.DMA((14,)),
            pltpu.SemaphoreType.DMA((7,)),
            pltpu.SemaphoreType.DMA((7,)),
            pltpu.SemaphoreType.DMA,
            pltpu.SemaphoreType.DMA,
            pltpu.SemaphoreType.DMA((7,)),
            pltpu.SemaphoreType.DMA,
            pltpu.SemaphoreType.DMA((32,)),
            pltpu.SemaphoreType.DMA,
            pltpu.SemaphoreType.DMA,
            pltpu.SemaphoreType.DMA,
            pltpu.SemaphoreType.REGULAR,
            pltpu.SemaphoreType.REGULAR,
        ],
        compiler_params=pltpu.CompilerParams(
            collective_id=0, has_side_effects=True, vmem_limit_bytes=40 << 20
        ),
        name="scores",
    )(
        *(
            pltpu.with_memory_space_constraint(array, pltpu.HBM)
            for array in (
                activations,
                out_grads,
                token_mask,
                proj_in.T,
                proj_out.T,
                inv_input,
                inv_output,
                query_feats,
            )
        )
    )
    return result.T


def solution(mesh):
    return jax.shard_map(
        local,
        mesh=mesh,
        in_specs=(
            P("ex", None, "hid"),
            P("ex", None, "hid"),
            P("ex", None),
            P("hid", None),
            P("hid", None),
            P(),
            P(),
            P("ex", "hid"),
        ),
        out_specs=P("ex", "hid"),
        check_vma=False,
    )
```

```python
import functools

import jax
import jax.numpy as jnp
from jax import lax
from jax.experimental import pallas as pl
from jax.experimental.pallas import tpu as pltpu
from jax.sharding import PartitionSpec as P

MESH = pl.DeviceIdType.MESH
F32 = jnp.float32
BF16 = jnp.bfloat16
IN_SENT, OUT_SENT = BF16, BF16
NT = (((1,), (1,)), ((), ()))
TN = (((0,), (0,)), ((), ()))
HIGHEST = lax.Precision.HIGHEST


def iota(shape, dim):
    return lax.broadcasted_iota(jnp.int32, shape, dim)


def kernel(
    act, grads, mask, proj_in, proj_out, inv_in, inv_out, query, out,
    act_v, grads_v, mask_v, win_v, wout_v, invin_v, invout_v, query_v,
    part_in, part_out, own_in, own_out, from_in, from_out, spread, qsend, qall, perm, feat, recv2,
    in_sem, send1_in, send1_out, got1_in, got1_out, sendq, gotq, send2, got2, send3, got3, met1, met2,
):
    ex, hid = lax.axis_index("ex"), lax.axis_index("hid")
    ylo, z, core = ex // 32, (ex // 2) % 16, ex % 2
    x, yhi = hid // 2, hid % 2

    def near(dy, dz):
        return (((ylo + dy) % 2) * 32 + ((z + dz + 16) % 16) * 2 + core, hid)

    def tell(sem, to):
        pl.semaphore_signal(sem, inc=1, device_id=to, device_id_type=MESH)

    other = (ex + 1 - 2 * core, hid)

    copies = []

    def load(src, dst):
        copy = pltpu.make_async_copy(src, dst, in_sem.at[len(copies)])
        copy.start()
        copies.append(copy)
        return copy

    def sequence(step):
        s = (x + step) % 4
        return [load(act.at[s], act_v.at[step]), load(grads.at[s], grads_v.at[step])]

    first = [copy for step in (2, 1) for copy in sequence(step)]
    loads = [load(proj_in, win_v), load(proj_out, wout_v)]

    barrier = pltpu.get_barrier_semaphore()
    for d in range(1, 8):
        tell(barrier, (ex, (hid + d) % 8))
    for d in (-4, -3, -2, -1, 1, 2, 3, 4):
        tell(barrier, near(0, d))
    tell(barrier, other)
    tell(barrier, near(1, 0))
    rest = [copy for step in (3, 0) for copy in sequence(step)]
    late = [load(inv_in, invin_v), load(inv_out, invout_v), load(query, query_v), load(mask, mask_v)]

    lane48 = iota((48, 128), 1)
    lane96 = iota((96, 128), 1)

    def project(step):
        win = jnp.concatenate([win_v[...]] * 2, axis=0)
        wout = jnp.concatenate([wout_v[:32]] * 4 + [wout_v[32:]] * 4, axis=0)
        y = lax.dot_general(act_v[step], win, NT, preferred_element_type=F32)
        packed = jnp.where(lane96 < 64, y[:96], y[96:])
        part_in[step] = packed.astype(IN_SENT)
        o = lax.dot_general(grads_v[step], wout, NT, preferred_element_type=F32)
        if step == 0:
            own_in[...] = packed
        for half in range(2):
            c = o[:, 128 * half : 128 * half + 128]
            picked = jnp.where(
                lane48 < 64,
                jnp.where(lane48 < 32, c[:48], c[48:96]),
                jnp.where(lane48 < 96, c[96:144], c[144:]),
            )
            part_out[step, half] = picked.astype(OUT_SENT)
            if step == 0:
                own_out[half] = picked

    def copy1(n):
        step, half = ((2, 0), (2, 1), (1, 0), (1, 1), (3, 0), (3, 1), (0, 1 - yhi))[n]
        to = ((x + step) % 4) * 2 + half
        at = (to - hid + 8) % 8 - 1
        return [
            pltpu.make_async_remote_copy(
                part_in.at[step], from_in.at[at], send1_in.at[n], got1_in, device_id=(ex, to), device_id_type=MESH
            ),
            pltpu.make_async_remote_copy(
                part_out.at[step, half], from_out.at[at], send1_out.at[n], got1_out,
                device_id=(ex, to), device_id_type=MESH,
            ),
        ]

    def start1(messages):
        for n in messages:
            for copy in copy1(n):
                copy.start()

    for copy in loads + first:
        copy.wait()
    for step in (2, 1):
        project(step)
    pl.semaphore_wait(barrier, 17)
    for d in (-4, -3, -2, -1, 1, 2, 3, 4):
        tell(met1, near(0, d))
    start1((0, 1, 2, 3))
    for copy in rest:
        copy.wait()
    for step in (3, 0):
        project(step)
    start1((4, 5, 6))

    def exact3(array):
        high = array.astype(BF16)
        left = array - high.astype(F32)
        middle = left.astype(BF16)
        return high, middle, (left - middle.astype(F32)).astype(BF16)

    for copy in late:
        copy.wait()
    m, col = iota((64, 128), 0), iota((64, 128), 1)
    place = m == 32 * (col // 64) + col % 32
    even = jnp.where(place & ((col // 32) % 2 == 0), 1.0, 0.0).astype(BF16)
    odd = jnp.where(place & ((col // 32) % 2 == 1), 1.0, 0.0).astype(BF16)
    both = jnp.concatenate(
        [
            jnp.dot(piece, where_to, preferred_element_type=F32).astype(BF16)
            for piece in exact3(invout_v[...])
            for where_to in (even, odd)
        ],
        axis=0,
    )
    pre = [
        jnp.dot(
            jnp.concatenate([query_v[:, 128 * b : 128 * b + 128]] * 3, axis=1), both, preferred_element_type=F32
        )
        for b in range(4)
    ]
    lane64 = iota((64, 128), 1)
    for b in range(2):
        left, right = pre[2 * b], pre[2 * b + 1]
        qsend[:, 128 * b : 128 * b + 128] = jnp.where(lane64 < 64, left, pltpu.roll(right, 64, 1)).astype(BF16)
        qsend[:, 256 + 128 * b : 384 + 128 * b] = jnp.where(
            lane64 < 64, pltpu.roll(left, 64, 1), right
        ).astype(BF16)
    qall[hid] = qsend[...]

    pl.semaphore_wait(met1, 8)
    for dy in range(2):
        for dz in (-4, 4):
            tell(met2, near(dy, dz))

    i, f = iota((64, 128), 0), iota((64, 128), 1)
    pieces = jnp.concatenate(exact3(invin_v[...]), axis=1)
    for k in range(16):
        pick = jnp.where(i == 4 * k + f // 32, 1.0, 0.0).astype(BF16)
        spread[k] = jnp.dot(pieces, jnp.concatenate([pick] * 3, axis=0), preferred_element_type=F32)
    r, c = iota((256, 256), 0), iota((256, 256), 1)
    perm[...] = jnp.where((c % 16 == r // 16) & (c // 16 == r % 16), 1.0, 0.0).astype(BF16)
    mask_row = mask_v[pl.ds(x, 1), :].astype(F32)
    count = jnp.sum(mask_row, axis=1, keepdims=True)
    t0, t1 = iota((48, 192), 0), iota((48, 192), 1)
    chosen = jnp.where(t1 % 48 == t0, 1.0, 0.0).astype(F32) * mask_row
    u0, u1 = iota((192, 128), 0), iota((192, 128), 1)
    group_of = jnp.where(u0 // 48 == u1 // 32, 1.0, 0.0).astype(BF16)
    weight = jnp.dot(chosen.astype(BF16), group_of, preferred_element_type=F32)

    def copyq(d):
        return pltpu.make_async_remote_copy(
            qsend, qall.at[hid], sendq.at[d - 1], gotq, device_id=(ex, (hid + d) % 8), device_id_type=MESH
        )


    pltpu.make_async_copy(from_out, from_out, got1_out).wait()
    pltpu.make_async_copy(from_in, from_in, got1_in).wait()
    side_in, side_out = own_in[...], own_out[yhi]
    for n in range(7):
        side_in = side_in + from_in[n].astype(F32)
        side_out = side_out + from_out[n].astype(F32)
    side_out = side_out * weight
    in_hi = side_in.astype(BF16)
    in_lo = (side_in - in_hi.astype(F32)).astype(BF16)
    out_hi = side_out.astype(BF16)
    out_lo = (side_out - out_hi.astype(F32)).astype(BF16)
    right = jnp.concatenate([out_hi, out_lo, out_hi], axis=0)
    first = lax.dot_general(
        jnp.concatenate([in_hi[:48], in_hi[:48], in_lo[:48]], axis=0), right, TN, preferred_element_type=F32
    )
    second = lax.dot_general(
        jnp.concatenate([in_hi[48:], in_hi[48:], in_lo[48:]], axis=0), right, TN, preferred_element_type=F32
    )
    outer = jnp.where(
        lane64 < 64,
        jnp.where(lane64 < 32, first[:64], second[:64]),
        jnp.where(lane64 < 96, first[64:], second[64:]),
    )
    outer = outer + pltpu.roll(outer, 64, 1)
    outer = outer + pltpu.roll(outer, 32, 1)
    mixed = jnp.concatenate([jnp.sum(spread[k] * outer, axis=0, keepdims=True) for k in range(16)], axis=0)
    feat[...] = (mixed / count).astype(BF16)

    home = ex // 8
    slot = (z % 4) * 4 + x
    early = [(0, dz) for dz in (4, 12, 3, 13, 2, 14, 1, 15)]
    order = early + [(dy, dz) for dz in (8, 7, 9, 6, 10, 5, 11, 4, 12, 3, 13, 2, 14, 1, 15, 0) for dy in (1, 0) if (dy, dz) not in early and (dy, dz) != (0, 0)] + [(0, 0)]

    def copy2(n):
        return pltpu.make_async_remote_copy(
            feat, recv2.at[0, yhi, slot], send2.at[n], got2,
            device_id=(near(*order[n])[0], home), device_id_type=MESH,
        )

    for n in range(len(early)):
        copy2(n).start()
    pl.semaphore_wait(met2, 4)
    for n in range(len(early), 31):
        copy2(n).start()

    @pl.when(hid != home)
    def _():
        copy2(31).start()

    @pl.when(hid == home)
    def _():
        pltpu.make_async_copy(feat, recv2.at[0, yhi, slot], got2).start()

    for d in range(1, 8):
        copyq(d).start()

    for n in range(7):
        for copy in copy1(n):
            copy.wait_send()
    for n in range(31):
        copy2(n).wait_send()

    @pl.when(hid != home)
    def _():
        copy2(31).wait_send()

    for d in range(1, 8):
        copyq(d).wait_send()
    pltpu.make_async_copy(recv2.at[0], recv2.at[0], got2).wait()

    copy3 = pltpu.make_async_remote_copy(
        recv2.at[0], recv2.at[1], send3, got3, device_id=other, device_id_type=MESH
    )
    copy3.start()
    pltpu.make_async_copy(qall.at[pl.ds(0, 7)], qall.at[pl.ds(0, 7)], gotq).wait()
    queries = jnp.concatenate([qall[h] for h in range(8)], axis=1)

    def scores(side):
        ordered = [
            jnp.dot(perm[...], recv2[side, half].reshape(256, 128), preferred_element_type=F32).astype(BF16)
            for half in range(2)
        ]
        lhs = jnp.concatenate(
            [
                ordered[half][32 * h + 16 * k : 32 * h + 16 * k + 16]
                for h in range(8)
                for half in range(2)
                for k in range(2)
            ],
            axis=1,
        )
        return lax.dot_general(lhs, queries, NT, preferred_element_type=F32)

    mine = scores(0)
    copy3.wait()
    theirs = scores(1)
    even = jnp.where(core == 0, mine, theirs)
    odd = jnp.where(core == 0, theirs, mine)
    for g in range(4):
        out[8 * g : 8 * g + 4, :] = even[4 * g : 4 * g + 4]
        out[8 * g + 4 : 8 * g + 8, :] = odd[4 * g : 4 * g + 4]


def local(activations, out_grads, token_mask, proj_in, proj_out, inv_input, inv_output, query_feats):
    hbm = pl.BlockSpec(memory_space=pltpu.HBM)
    result = pl.pallas_call(
        kernel,
        out_shape=jax.ShapeDtypeStruct((32, 64), F32),
        in_specs=[hbm] * 8,
        out_specs=pl.BlockSpec(memory_space=pltpu.VMEM),
        scratch_shapes=[
            pltpu.VMEM((4, 192, 1792), BF16),
            pltpu.VMEM((4, 192, 512), BF16),
            pltpu.VMEM((4, 192), jnp.int32),
            pltpu.VMEM((64, 1792), BF16),
            pltpu.VMEM((64, 512), BF16),
            pltpu.VMEM((64, 64), F32),
            pltpu.VMEM((64, 64), F32),
            pltpu.VMEM((64, 512), BF16),
            pltpu.VMEM((4, 96, 128), IN_SENT),
            pltpu.VMEM((4, 2, 48, 128), OUT_SENT),
            pltpu.VMEM((96, 128), F32),
            pltpu.VMEM((2, 48, 128), F32),
            pltpu.VMEM((7, 96, 128), IN_SENT),
            pltpu.VMEM((7, 48, 128), OUT_SENT),
            pltpu.VMEM((16, 64, 128), F32),
            pltpu.VMEM((64, 512), BF16),
            pltpu.VMEM((8, 64, 512), BF16),
            pltpu.VMEM((256, 256), BF16),
            pltpu.VMEM((16, 128), BF16),
            pltpu.VMEM((2, 2, 16, 16, 128), BF16),
            pltpu.SemaphoreType.DMA((14,)),
            pltpu.SemaphoreType.DMA((7,)),
            pltpu.SemaphoreType.DMA((7,)),
            pltpu.SemaphoreType.DMA,
            pltpu.SemaphoreType.DMA,
            pltpu.SemaphoreType.DMA((7,)),
            pltpu.SemaphoreType.DMA,
            pltpu.SemaphoreType.DMA((32,)),
            pltpu.SemaphoreType.DMA,
            pltpu.SemaphoreType.DMA,
            pltpu.SemaphoreType.DMA,
            pltpu.SemaphoreType.REGULAR,
            pltpu.SemaphoreType.REGULAR,
        ],
        compiler_params=pltpu.CompilerParams(
            collective_id=0, has_side_effects=True, vmem_limit_bytes=40 << 20
        ),
        name="scores",
    )(
        *(
            pltpu.with_memory_space_constraint(array, pltpu.HBM)
            for array in (
                activations,
                out_grads,
                token_mask,
                proj_in.T,
                proj_out.T,
                inv_input,
                inv_output,
                query_feats,
            )
        )
    )
    return result.T


def solution(mesh):
    return jax.shard_map(
        local,
        mesh=mesh,
        in_specs=(
            P("ex", None, "hid"),
            P("ex", None, "hid"),
            P("ex", None),
            P("hid", None),
            P("hid", None),
            P(),
            P(),
            P("ex", "hid"),
        ),
        out_specs=P("ex", "hid"),
        check_vma=False,
    )
```

```python
import functools

import jax
import jax.numpy as jnp
from jax import lax
from jax.experimental import pallas as pl
from jax.experimental.pallas import tpu as pltpu
from jax.sharding import PartitionSpec as P

MESH = pl.DeviceIdType.MESH
F32 = jnp.float32
BF16 = jnp.bfloat16
IN_SENT, OUT_SENT = BF16, BF16
NT = (((1,), (1,)), ((), ()))
TN = (((0,), (0,)), ((), ()))
HIGHEST = lax.Precision.HIGHEST


def iota(shape, dim):
    return lax.broadcasted_iota(jnp.int32, shape, dim)


def kernel(
    act, grads, mask, proj_in, proj_out, inv_in, inv_out, query, out,
    act_v, grads_v, mask_v, win_v, wout_v, invin_v, invout_v, query_v,
    part_in, part_out, own_in, own_out, from_in, from_out, spread, qsend, qall, perm, feat, recv2,
    in_sem, send1_in, send1_out, got1_in, got1_out, sendq, gotq, send2, got2, send3, got3, met1, met2,
):
    ex, hid = lax.axis_index("ex"), lax.axis_index("hid")
    ylo, z, core = ex // 32, (ex // 2) % 16, ex % 2
    x, yhi = hid // 2, hid % 2

    def near(dy, dz):
        return (((ylo + dy) % 2) * 32 + ((z + dz + 16) % 16) * 2 + core, hid)

    def tell(sem, to):
        pl.semaphore_signal(sem, inc=1, device_id=to, device_id_type=MESH)

    other = (ex + 1 - 2 * core, hid)

    copies = []

    def load(src, dst):
        copy = pltpu.make_async_copy(src, dst, in_sem.at[len(copies)])
        copy.start()
        copies.append(copy)
        return copy

    def sequence(step):
        s = (x + step) % 4
        return [load(act.at[s], act_v.at[step]), load(grads.at[s], grads_v.at[step])]

    first = [copy for step in (2, 1) for copy in sequence(step)]
    loads = [load(proj_in, win_v), load(proj_out, wout_v)]

    barrier = pltpu.get_barrier_semaphore()
    for d in range(1, 8):
        tell(barrier, (ex, (hid + d) % 8))
    for d in (-4, -3, -2, -1, 1, 2, 3, 4):
        tell(barrier, near(0, d))
    tell(barrier, other)
    tell(barrier, near(1, 0))
    rest = [copy for step in (3, 0) for copy in sequence(step)]
    late = [load(inv_in, invin_v), load(inv_out, invout_v), load(query, query_v), load(mask, mask_v)]

    lane48 = iota((48, 128), 1)
    lane96 = iota((96, 128), 1)

    def project(step):
        win = jnp.concatenate([win_v[...]] * 2, axis=0)
        wout = jnp.concatenate([wout_v[:32]] * 4 + [wout_v[32:]] * 4, axis=0)
        y = lax.dot_general(act_v[step], win, NT, preferred_element_type=F32)
        packed = jnp.where(lane96 < 64, y[:96], y[96:])
        part_in[step] = packed.astype(IN_SENT)
        o = lax.dot_general(grads_v[step], wout, NT, preferred_element_type=F32)
        if step == 0:
            own_in[...] = packed
        for half in range(2):
            c = o[:, 128 * half : 128 * half + 128]
            picked = jnp.where(
                lane48 < 64,
                jnp.where(lane48 < 32, c[:48], c[48:96]),
                jnp.where(lane48 < 96, c[96:144], c[144:]),
            )
            part_out[step, half] = picked.astype(OUT_SENT)
            if step == 0:
                own_out[half] = picked

    def copy1(n):
        step, half = ((2, 0), (2, 1), (1, 0), (1, 1), (3, 0), (3, 1), (0, 1 - yhi))[n]
        to = ((x + step) % 4) * 2 + half
        at = (to - hid + 8) % 8 - 1
        return [
            pltpu.make_async_remote_copy(
                part_in.at[step], from_in.at[at], send1_in.at[n], got1_in, device_id=(ex, to), device_id_type=MESH
            ),
            pltpu.make_async_remote_copy(
                part_out.at[step, half], from_out.at[at], send1_out.at[n], got1_out,
                device_id=(ex, to), device_id_type=MESH,
            ),
        ]

    def start1(messages):
        for n in messages:
            for copy in copy1(n):
                copy.start()

    for copy in loads + first:
        copy.wait()
    for step in (2, 1):
        project(step)
    pl.semaphore_wait(barrier, 17)
    for d in (-4, -3, -2, -1, 1, 2, 3, 4):
        tell(met1, near(0, d))
    start1((0, 1, 2, 3))
    for copy in rest:
        copy.wait()
    for step in (3, 0):
        project(step)
    start1((4, 5, 6))

    def exact3(array):
        high = array.astype(BF16)
        left = array - high.astype(F32)
        middle = left.astype(BF16)
        return high, middle, (left - middle.astype(F32)).astype(BF16)

    for copy in late:
        copy.wait()
    m, col = iota((64, 128), 0), iota((64, 128), 1)
    place = m == 32 * (col // 64) + col % 32
    even = jnp.where(place & ((col // 32) % 2 == 0), 1.0, 0.0).astype(BF16)
    odd = jnp.where(place & ((col // 32) % 2 == 1), 1.0, 0.0).astype(BF16)
    both = jnp.concatenate(
        [
            jnp.dot(piece, where_to, preferred_element_type=F32).astype(BF16)
            for piece in exact3(invout_v[...])
            for where_to in (even, odd)
        ],
        axis=0,
    )
    pre = [
        jnp.dot(
            jnp.concatenate([query_v[:, 128 * b : 128 * b + 128]] * 3, axis=1), both, preferred_element_type=F32
        )
        for b in range(4)
    ]
    lane64 = iota((64, 128), 1)
    for b in range(2):
        left, right = pre[2 * b], pre[2 * b + 1]
        qsend[:, 128 * b : 128 * b + 128] = jnp.where(lane64 < 64, left, pltpu.roll(right, 64, 1)).astype(BF16)
        qsend[:, 256 + 128 * b : 384 + 128 * b] = jnp.where(
            lane64 < 64, pltpu.roll(left, 64, 1), right
        ).astype(BF16)
    qall[hid] = qsend[...]

    pl.semaphore_wait(met1, 8)
    for dy in range(2):
        for dz in (-4, 4):
            tell(met2, near(dy, dz))

    i, f = iota((64, 128), 0), iota((64, 128), 1)
    pieces = jnp.concatenate(exact3(invin_v[...]), axis=1)
    for k in range(16):
        pick = jnp.where(i == 4 * k + f // 32, 1.0, 0.0).astype(BF16)
        spread[k] = jnp.dot(pieces, jnp.concatenate([pick] * 3, axis=0), preferred_element_type=F32)
    r, c = iota((256, 256), 0), iota((256, 256), 1)
    perm[...] = jnp.where((c % 16 == r // 16) & (c // 16 == r % 16), 1.0, 0.0).astype(BF16)
    mask_row = mask_v[pl.ds(x, 1), :].astype(F32)
    count = jnp.sum(mask_row, axis=1, keepdims=True)
    t0, t1 = iota((48, 192), 0), iota((48, 192), 1)
    chosen = jnp.where(t1 % 48 == t0, 1.0, 0.0).astype(F32) * mask_row
    u0, u1 = iota((192, 128), 0), iota((192, 128), 1)
    group_of = jnp.where(u0 // 48 == u1 // 32, 1.0, 0.0).astype(BF16)
    weight = jnp.dot(chosen.astype(BF16), group_of, preferred_element_type=F32)

    def copyq(d):
        return pltpu.make_async_remote_copy(
            qsend, qall.at[hid], sendq.at[d - 1], gotq, device_id=(ex, (hid + d) % 8), device_id_type=MESH
        )


    pltpu.make_async_copy(from_out, from_out, got1_out).wait()
    pltpu.make_async_copy(from_in, from_in, got1_in).wait()
    side_in, side_out = own_in[...], own_out[yhi]
    for n in range(7):
        side_in = side_in + from_in[n].astype(F32)
        side_out = side_out + from_out[n].astype(F32)
    side_out = side_out * weight
    in_hi = side_in.astype(BF16)
    in_lo = (side_in - in_hi.astype(F32)).astype(BF16)
    out_hi = side_out.astype(BF16)
    out_lo = (side_out - out_hi.astype(F32)).astype(BF16)
    right = jnp.concatenate([out_hi, out_lo, out_hi], axis=0)
    first = lax.dot_general(
        jnp.concatenate([in_hi[:48], in_hi[:48], in_lo[:48]], axis=0), right, TN, preferred_element_type=F32
    )
    second = lax.dot_general(
        jnp.concatenate([in_hi[48:], in_hi[48:], in_lo[48:]], axis=0), right, TN, preferred_element_type=F32
    )
    outer = jnp.where(
        lane64 < 64,
        jnp.where(lane64 < 32, first[:64], second[:64]),
        jnp.where(lane64 < 96, first[64:], second[64:]),
    )
    outer = outer + pltpu.roll(outer, 64, 1)
    outer = outer + pltpu.roll(outer, 32, 1)
    mixed = jnp.concatenate([jnp.sum(spread[k] * outer, axis=0, keepdims=True) for k in range(16)], axis=0)
    feat[...] = (mixed / count).astype(BF16)

    home = ex // 8
    slot = (z % 4) * 4 + x
    early = [(0, dz) for dz in (4, 12, 3, 13, 2, 14, 1, 15)]
    order = early + [(dy, dz) for dz in (8, 7, 9, 6, 10, 5, 11, 4, 12, 3, 13, 2, 14, 1, 15, 0) for dy in (1, 0) if (dy, dz) not in early and (dy, dz) != (0, 0)] + [(0, 0)]

    def copy2(n):
        return pltpu.make_async_remote_copy(
            feat, recv2.at[0, yhi, slot], send2.at[n], got2,
            device_id=(near(*order[n])[0], home), device_id_type=MESH,
        )

    for n in range(len(early)):
        copy2(n).start()
    pl.semaphore_wait(met2, 4)
    for n in range(len(early), 31):
        copy2(n).start()

    @pl.when(hid != home)
    def _():
        copy2(31).start()

    @pl.when(hid == home)
    def _():
        pltpu.make_async_copy(feat, recv2.at[0, yhi, slot], got2).start()

    for d in range(1, 8):
        copyq(d).start()

    pltpu.make_async_copy(recv2.at[0], recv2.at[0], got2).wait()

    copy3 = pltpu.make_async_remote_copy(
        recv2.at[0], recv2.at[1], send3, got3, device_id=other, device_id_type=MESH
    )
    copy3.start()
    pltpu.make_async_copy(qall.at[pl.ds(0, 7)], qall.at[pl.ds(0, 7)], gotq).wait()
    queries = jnp.concatenate([qall[h] for h in range(8)], axis=1)

    def scores(side):
        ordered = [
            jnp.dot(perm[...], recv2[side, half].reshape(256, 128), preferred_element_type=F32).astype(BF16)
            for half in range(2)
        ]
        lhs = jnp.concatenate(
            [
                ordered[half][32 * h + 16 * k : 32 * h + 16 * k + 16]
                for h in range(8)
                for half in range(2)
                for k in range(2)
            ],
            axis=1,
        )
        return lax.dot_general(lhs, queries, NT, preferred_element_type=F32)

    mine = scores(0)
    copy3.wait()
    theirs = scores(1)
    even = jnp.where(core == 0, mine, theirs)
    odd = jnp.where(core == 0, theirs, mine)
    for g in range(4):
        out[8 * g : 8 * g + 4, :] = even[4 * g : 4 * g + 4]
        out[8 * g + 4 : 8 * g + 8, :] = odd[4 * g : 4 * g + 4]

    for n in range(7):
        for copy in copy1(n):
            copy.wait_send()
    for n in range(31):
        copy2(n).wait_send()

    @pl.when(hid != home)
    def _():
        copy2(31).wait_send()

    for d in range(1, 8):
        copyq(d).wait_send()


def local(activations, out_grads, token_mask, proj_in, proj_out, inv_input, inv_output, query_feats):
    hbm = pl.BlockSpec(memory_space=pltpu.HBM)
    result = pl.pallas_call(
        kernel,
        out_shape=jax.ShapeDtypeStruct((32, 64), F32),
        in_specs=[hbm] * 8,
        out_specs=pl.BlockSpec(memory_space=pltpu.VMEM),
        scratch_shapes=[
            pltpu.VMEM((4, 192, 1792), BF16),
            pltpu.VMEM((4, 192, 512), BF16),
            pltpu.VMEM((4, 192), jnp.int32),
            pltpu.VMEM((64, 1792), BF16),
            pltpu.VMEM((64, 512), BF16),
            pltpu.VMEM((64, 64), F32),
            pltpu.VMEM((64, 64), F32),
            pltpu.VMEM((64, 512), BF16),
            pltpu.VMEM((4, 96, 128), IN_SENT),
            pltpu.VMEM((4, 2, 48, 128), OUT_SENT),
            pltpu.VMEM((96, 128), F32),
            pltpu.VMEM((2, 48, 128), F32),
            pltpu.VMEM((7, 96, 128), IN_SENT),
            pltpu.VMEM((7, 48, 128), OUT_SENT),
            pltpu.VMEM((16, 64, 128), F32),
            pltpu.VMEM((64, 512), BF16),
            pltpu.VMEM((8, 64, 512), BF16),
            pltpu.VMEM((256, 256), BF16),
            pltpu.VMEM((16, 128), BF16),
            pltpu.VMEM((2, 2, 16, 16, 128), BF16),
            pltpu.SemaphoreType.DMA((14,)),
            pltpu.SemaphoreType.DMA((7,)),
            pltpu.SemaphoreType.DMA((7,)),
            pltpu.SemaphoreType.DMA,
            pltpu.SemaphoreType.DMA,
            pltpu.SemaphoreType.DMA((7,)),
            pltpu.SemaphoreType.DMA,
            pltpu.SemaphoreType.DMA((32,)),
            pltpu.SemaphoreType.DMA,
            pltpu.SemaphoreType.DMA,
            pltpu.SemaphoreType.DMA,
            pltpu.SemaphoreType.REGULAR,
            pltpu.SemaphoreType.REGULAR,
        ],
        compiler_params=pltpu.CompilerParams(
            collective_id=0, has_side_effects=True, vmem_limit_bytes=40 << 20
        ),
        name="scores",
    )(
        *(
            pltpu.with_memory_space_constraint(array, pltpu.HBM)
            for array in (
                activations,
                out_grads,
                token_mask,
                proj_in.T,
                proj_out.T,
                inv_input,
                inv_output,
                query_feats,
            )
        )
    )
    return result.T


def solution(mesh):
    return jax.shard_map(
        local,
        mesh=mesh,
        in_specs=(
            P("ex", None, "hid"),
            P("ex", None, "hid"),
            P("ex", None),
            P("hid", None),
            P("hid", None),
            P(),
            P(),
            P("ex", "hid"),
        ),
        out_specs=P("ex", "hid"),
        check_vma=False,
    )
```
